128 devices in a mesh: spin: 8 (over y, core), fock: 16 (over x, z).
Axes of the slice: x: 4, y: 4, z: 4, core: 2. Of those that a mesh axis runs over, the one named last changes fastest.
Arguments:
- amplitudes: float32 [2, 8192, 8192], P(None, 'spin', 'fock'), may hold values from -6 to 6
- cutoffs: int32 [8192], P('spin'), may hold values from 256 to 512
- coupling_first: float32 [13], replicated, may hold values from 0.05 to 0.5
- coupling_second: float32 [13], replicated, may hold values from 0.2 to 2
- frozen_coupling: float32 [16], replicated, may hold values from 1 to 4
- frozen_bits: int32 [16], replicated, may hold values from 0 to 1, as said below
- drive_bits: int32 [13], replicated, may hold values 0 or 1
- angles: float32 [13], replicated, may hold values from 0.3 to 1.3
Outputs:
- evolved: float32 [2, 8192, 8192], P(None, 'spin', 'fock')
The draws below stay inside these ranges and needn't reach their ends.
Inputs may be any that keep to these rules, and one draw needn't show every extreme that they name: `cutoffs`: highest level plus one of the first mode that the ladder couples in each spin configuration. `frozen_bits`: between one and four frozen spins have bit 1, the others bit 0.
All inputs are finite; a program needn't handle non-finite values.
Results may differ from the reference program's by a relative error of at most 0.0003.
Values sent between devices are 32-bit elements; how exact they have to be, the bound alone decides.
A program may use at most 192 MiB of HBM per device.

```python
import math
import jax
import jax.numpy as jnp
from jax import lax

SPINS = 13
FA = 512
FB = 16
FROZEN = 16
DEGREE = 16
CONFIGS = 8192
COLUMNS = 8192


def draw_frozen_bits(key, part):
    keys = jax.random.split(key, 2)
    most_flipped = max(1, FROZEN // 4)
    flipped = jax.random.randint(keys[0], (), 1, most_flipped + 1)
    scores = jax.random.randint(keys[1], (FROZEN,), 0, 1 << 20) * FROZEN + jnp.arange(FROZEN, dtype=jnp.int32)
    ranks = jnp.argsort(jnp.argsort(scores, stable=True), stable=True)
    return (ranks < flipped).astype(jnp.int32)


def with_ends(drawn, own_key, low, high):
    dims = drawn.shape
    spot = [jax.random.randint(jax.random.fold_in(own_key, axis), (), 0, dims[axis]) for axis in range(len(dims))]
    drawn = drawn.at[tuple(spot)].set(low)
    longest = dims.index(max(dims))
    spot[longest] = (spot[longest] + 1) % dims[longest]
    return drawn.at[tuple(spot)].set(high)


def level_of(stream_key, dims, cuts, smallest, top_value):
    factor_of, own = 1.0, jax.random.fold_in(stream_key, 6)
    for position, blocks in cuts:
        heights = jnp.exp(jax.random.uniform(jax.random.fold_in(own, position), (blocks,), jnp.float32, smallest / len(cuts), top_value / len(cuts)))
        factor_of = factor_of * jnp.repeat(heights, dims[position] // blocks).reshape([-1 if axis == position else 1 for axis in range(len(dims))])
    return factor_of


def centred(key, dims, deviation, reach, cuts=(), kind=jnp.bfloat16):
    entries = jax.random.normal(key, dims, jnp.float32) * deviation
    if len(cuts) > 0:
        entries = level_of(key, dims, cuts, -0.22, 0.18) * entries
    return jnp.clip(entries, min=-reach, max=reach).astype(kind)


def setup_inputs(seed: int = 0) -> dict:
    arg_keys = jax.random.split(jax.random.key(seed), 9)
    return {
        "amplitudes": centred(arg_keys[0], (2, CONFIGS, COLUMNS), 1.0, 6.0, ((1, 8), (2, 16)), jnp.float32),
        "cutoffs": with_ends(jax.random.randint(arg_keys[1], (CONFIGS,), FA // 2, FA + 1), jax.random.fold_in(arg_keys[1], 1), FA // 2, FA).astype(jnp.int32),
        "coupling_first": jnp.clip(jnp.exp(jax.random.uniform(arg_keys[2], (SPINS,), jnp.float32, math.log(0.05), math.log(0.5))), 0.05, 0.5),
        "coupling_second": jnp.clip(jnp.exp(jax.random.uniform(arg_keys[3], (SPINS,), jnp.float32, math.log(0.2), math.log(2.0))), 0.2, 2.0),
        "frozen_coupling": jnp.clip(jnp.exp(jax.random.uniform(arg_keys[4], (FROZEN,), jnp.float32, math.log(1.0), math.log(4.0))), 1.0, 4.0),
        "frozen_bits": draw_frozen_bits(jax.random.fold_in(arg_keys[8], 71), 0),
        "drive_bits": with_ends((jax.random.randint(arg_keys[6], (SPINS,), 0, 2) < 1).astype(jnp.int32), jax.random.fold_in(arg_keys[6], 1), 0, 1),
        "angles": jnp.clip(jax.random.uniform(arg_keys[7], (SPINS,), jnp.float32, 0.3, 1.3), 0.3, 1.3),
    }


evolve_time = 12.0
diagonal_first = 0.06
diagonal_second = 0.04
ladder_first = 0.35
ladder_second = 0.1

def bessel_first(term_order, argument):
    running = 0.0
    addend = (argument / 2.0) ** term_order / math.factorial(term_order)
    for serial in range(80):
        running = running + addend
        addend = addend * -(argument * argument / 4.0) / ((serial + 1) * (serial + 1 + term_order))
    return running

def coefficient_table(term_count):
    real_table = []
    imag_table = []
    for term_order in range(term_count + 1):
        magnitude = (1.0 if term_order == 0 else 2.0) * bessel_first(term_order, evolve_time)
        quarter = term_order % 4
        real_table.append(magnitude if quarter == 0 else -magnitude if quarter == 2 else 0.0)
        imag_table.append(-magnitude if quarter == 1 else magnitude if quarter == 3 else 0.0)
    return (real_table, imag_table)

def spin_strengths(config_index, coupling_first, coupling_second, frozen_coupling, frozen_bits):
    spin_bits = config_index[:, None] >> jnp.arange(SPINS, dtype=jnp.int32)[None, :] & 1
    spin_signs = (1 - 2 * spin_bits).astype(jnp.float32)
    frozen_signs = (1 - 2 * frozen_bits).astype(jnp.float32)
    frozen_part = jnp.sum(frozen_coupling * frozen_signs)
    total_first = jnp.sum(coupling_first) + jnp.sum(frozen_coupling)
    strength_first = ladder_first * (lax.optimization_barrier(jnp.sum(spin_signs * coupling_first[None, :], axis=1)) + frozen_part) / total_first
    strength_second = ladder_second * lax.optimization_barrier(jnp.sum(spin_signs * coupling_second[None, :], axis=1)) / jnp.sum(coupling_second)
    return (strength_first, strength_second)

def apply_hamiltonian(padded, first_level, strength_first, strength_second, cutoff_rows):
    column_count = padded.shape[2] - 2 * FB
    center = padded[:, :, FB:FB + column_count]
    lower_level = padded[:, :, :column_count]
    upper_level = padded[:, :, 2 * FB:]
    column = lax.broadcasted_iota(jnp.int32, (1, column_count), 1)
    level_index = first_level + column // FB
    sub_index = column % FB
    cutoff = cutoff_rows[:, None]
    level_float = level_index.astype(jnp.float32)
    sub_float = sub_index.astype(jnp.float32)
    mode_low = jnp.where((level_index >= 1) & (level_index < cutoff), jnp.sqrt(jnp.maximum(level_float, 0.0) / FA), 0.0)
    mode_high = jnp.where((level_index + 1 >= 1) & (level_index + 1 < cutoff), jnp.sqrt(jnp.maximum(level_float + 1.0, 0.0) / FA), 0.0)
    sub_low = jnp.sqrt(sub_float / FB)
    sub_high = jnp.where(sub_index + 1 < FB, jnp.sqrt((sub_float + 1.0) / FB), 0.0)
    diagonal = diagonal_first * (2.0 * level_float / (FA - 1) - 1.0) + diagonal_second * (2.0 * sub_float / (FB - 1) - 1.0)
    previous_sub = jnp.pad(center[:, :, :-1], ((0, 0), (0, 0), (1, 0)))
    next_sub = jnp.pad(center[:, :, 1:], ((0, 0), (0, 0), (0, 1)))
    first_term = strength_first[None, :, None] * (mode_low[None] * lower_level + mode_high[None] * upper_level)
    second_term = strength_second[None, :, None] * (sub_low[None] * previous_sub + sub_high[None] * next_sub)
    return diagonal[None] * center + first_term + second_term

def weighted_term(term_vector, real_weight, imag_weight):
    rotated = jnp.stack([-term_vector[1], term_vector[0]])
    return real_weight * term_vector + imag_weight * rotated

def chebyshev_series(vector, apply_operator, term_count):
    real_table, imag_table = coefficient_table(term_count)
    real_weights = jnp.asarray(real_table, dtype=jnp.float32)
    imag_weights = jnp.asarray(imag_table, dtype=jnp.float32)
    current = apply_operator(vector)
    running = weighted_term(vector, real_weights[0], imag_weights[0]) + weighted_term(current, real_weights[1], imag_weights[1])

    def advance(term_index, loop_state):
        previous, present, total = loop_state
        following = 2.0 * apply_operator(present) - previous
        total = total + weighted_term(following, real_weights[term_index], imag_weights[term_index])
        return (present, following, total)
    loop_state = lax.fori_loop(2, term_count + 1, advance, (vector, current, running))
    return loop_state[2]

def partner_term(own_part, partner, cosine, sine_value, phase_bit, side_sign):
    keep_part = 1.0 - phase_bit
    real_part = cosine * own_part[0] + sine_value * (side_sign * phase_bit * partner[0] + keep_part * partner[1])
    imag_part = cosine * own_part[1] + sine_value * (side_sign * phase_bit * partner[1] - keep_part * partner[0])
    return jnp.stack([real_part, imag_part])

def rotate_bits(vector, bit_list, angles, drive_bits):
    cosines = jnp.cos(angles)
    sine_values = jnp.sin(angles)
    phases = drive_bits.astype(jnp.float32)
    for spin_slot, bit_number in bit_list:
        config_total = vector.shape[1]
        lower_size = 1 << bit_number
        shaped = vector.reshape(2, config_total // (2 * lower_size), 2, lower_size, vector.shape[2])
        lower_half = shaped[:, :, 0]
        upper_half = shaped[:, :, 1]
        new_lower = partner_term(lower_half, upper_half, cosines[spin_slot], sine_values[spin_slot], phases[spin_slot], -1.0)
        new_upper = partner_term(upper_half, lower_half, cosines[spin_slot], sine_values[spin_slot], phases[spin_slot], 1.0)
        vector = jnp.stack([new_lower, new_upper], axis=2).reshape(vector.shape)
    return vector

def reference(amplitudes, cutoffs, coupling_first, coupling_second, frozen_coupling, frozen_bits, drive_bits, angles):
    block_size = min(CONFIGS, 256)
    blocks = CONFIGS // block_size
    config_index = jnp.arange(CONFIGS, dtype=jnp.int32)
    strength_first, strength_second = spin_strengths(config_index, coupling_first, coupling_second, frozen_coupling, frozen_bits)
    stacked = amplitudes.reshape(2, blocks, block_size, COLUMNS).transpose(1, 0, 2, 3)

    def evolve_block(inputs):
        vector, block_first, block_second, block_cutoff = inputs

        def apply_operator(field):
            padded = jnp.pad(field, ((0, 0), (0, 0), (FB, FB)))
            return apply_hamiltonian(padded, 0, block_first, block_second, block_cutoff)
        return chebyshev_series(vector, apply_operator, DEGREE)
    evolved_blocks = lax.map(evolve_block, (stacked, strength_first.reshape(blocks, block_size), strength_second.reshape(blocks, block_size), cutoffs.reshape(blocks, block_size)))
    propagated = evolved_blocks.transpose(1, 0, 2, 3).reshape(2, CONFIGS, COLUMNS)
    return rotate_bits(propagated, [(slot, slot) for slot in range(SPINS)], angles, drive_bits)
```

```python
import math

import jax
import jax.numpy as jnp
from jax import lax
from jax.experimental import pallas as pl
from jax.experimental.pallas import tpu as pltpu
from jax.sharding import PartitionSpec as P

SPINS = 13
FA = 512
FB = 16
FROZEN = 16
DEGREE = 16
MESH_ID = pl.DeviceIdType.MESH

evolve_time = 12.0
diagonal_first = 0.06
diagonal_second = 0.04
ladder_first = 0.35
ladder_second = 0.1

PLACES = 8
CHUNKS = 8
GROUP = 16
LANES = PLACES * GROUP
OWN = 32
HALO = DEGREE
LEVELS = OWN + 2 * HALO
PADDED = LEVELS + 4
COLS = OWN * FB
SIDE = HALO * FB
LANE_BITS = (0, 1, 2, 3, 10, 11, 12)
AHEAD = 2


def bessel_first(term_order, argument):
    running = 0.0
    addend = (argument / 2.0) ** term_order / math.factorial(term_order)
    for serial in range(80):
        running = running + addend
        addend = addend * -(argument * argument / 4.0) / ((serial + 1) * (serial + 1 + term_order))
    return running


OMEGA = [(1.0 if k == 0 else 2.0) * bessel_first(k, evolve_time) for k in range(DEGREE + 1)]


def iota(shape, dim):
    return lax.broadcasted_iota(jnp.int32, shape, dim)


def fill_rotations(angles, drive_bits, rot):
    for j in range(SPINS):
        angle = jnp.full((8, 128), angles[j], jnp.float32)
        phase = jnp.full((8, 128), drive_bits[j], jnp.int32).astype(jnp.float32)
        sine = jnp.sin(angle)
        rot[3 * j] = jnp.cos(angle)
        rot[3 * j + 1] = sine * phase
        rot[3 * j + 2] = sine * (1.0 - phase)


def fill_mixer(rot, mix_hi, mix_lo):
    def rows(step, carry):
        base = pl.multiple_of(step * 16, 16)
        out_lane = base + iota((16, 128), 0)
        in_lane = iota((16, 128), 1)
        real = jnp.ones((16, 128), jnp.float32)
        imag = jnp.zeros((16, 128), jnp.float32)
        for place, bit in enumerate(LANE_BITS):
            out_bit = (out_lane >> place) & 1
            in_bit = (in_lane >> place) & 1
            same = out_bit == in_bit
            cosine = jnp.concatenate([rot[3 * bit]] * 2, axis=0)
            driven = jnp.concatenate([rot[3 * bit + 1]] * 2, axis=0)
            kept = jnp.concatenate([rot[3 * bit + 2]] * 2, axis=0)
            f_real = jnp.where(same, cosine, jnp.where(out_bit == 1, driven, -driven))
            f_imag = jnp.where(same, 0.0, -kept)
            real, imag = real * f_real - imag * f_imag, real * f_imag + imag * f_real
        top = jnp.concatenate([real, -imag], axis=1)
        low = jnp.concatenate([imag, real], axis=1)
        for start, value in ((0, top), (128, low)):
            high = value.astype(jnp.bfloat16)
            rest = (value - high.astype(jnp.float32)).astype(jnp.bfloat16)
            mix_hi[pl.ds(start + base, 16), :] = high
            mix_lo[pl.ds(start + base, 16), :] = rest
        return carry

    lax.fori_loop(0, 8, rows, 0)


def fill_diagonal(fock_place, diag):
    def rows(n, carry):
        row = iota((16, 128), 0)
        m = 2 * (row % 8) + row // 8
        level = fock_place * OWN - HALO + n
        level_float = jnp.full((16, 128), level, jnp.int32).astype(jnp.float32)
        value = diagonal_first * (2.0 * level_float / (FA - 1) - 1.0) + diagonal_second * (
            2.0 * m.astype(jnp.float32) / (FB - 1) - 1.0
        )
        diag[pl.ds(pl.multiple_of(n * 16, 16), 16), :] = 2.0 * value
        return carry

    lax.fori_loop(0, PADDED, rows, 0)


def strengths(chunk, spin_place, coupling_first, coupling_second, frozen_coupling, frozen_bits):
    shape = (8, 128)
    lane = iota(shape, 1)
    config = (lane >> 4) * 1024 + (spin_place * CHUNKS + chunk) * GROUP + (lane & 15)
    first = jnp.zeros(shape, jnp.float32)
    second = jnp.zeros(shape, jnp.float32)
    total_first = jnp.zeros(shape, jnp.float32)
    total_second = jnp.zeros(shape, jnp.float32)
    for j in range(SPINS):
        sign = (1 - 2 * ((config >> j) & 1)).astype(jnp.float32)
        first = first + coupling_first[j] * sign
        second = second + coupling_second[j] * sign
        total_first = total_first + coupling_first[j]
        total_second = total_second + coupling_second[j]
    for k in range(FROZEN):
        sign = jnp.full(shape, 1 - 2 * frozen_bits[k], jnp.int32).astype(jnp.float32)
        first = first + frozen_coupling[k] * sign
        total_first = total_first + frozen_coupling[k]
    return ladder_first * first / total_first, ladder_second * second / total_second


def butterfly(real, imag, rot, bits):
    count = len(real)
    for place, bit in enumerate(bits):
        cosine, driven, kept = rot[3 * bit], rot[3 * bit + 1], rot[3 * bit + 2]
        step = 1 << place
        for low in range(count):
            if low & step:
                continue
            up = low | step
            lr, li, ur, ui = real[low], imag[low], real[up], imag[up]
            real[low] = cosine * lr - driven * ur + kept * ui
            imag[low] = cosine * li - driven * ui - kept * ur
            real[up] = cosine * ur + driven * lr + kept * li
            imag[up] = cosine * ui + driven * li - kept * lr
    return real, imag


def kernel(
    x,
    cutoffs,
    coupling_first,
    coupling_second,
    frozen_coupling,
    frozen_bits,
    drive_bits,
    angles,
    out,
    inb,
    cut_all,
    left,
    right,
    nat_re,
    nat_im,
    vec_re,
    vec_im,
    even_re,
    even_im,
    odd_re,
    odd_im,
    y_re,
    y_im,
    diag,
    ladder,
    rot,
    mix_hi,
    mix_lo,
    outb,
    back,
    in_send,
    in_recv,
    cut_send,
    cut_recv,
    halo_send,
    halo_recv,
    out_send,
    out_recv,
    store_sem,
):
    s = lax.axis_index("spin")
    f = lax.axis_index("fock")
    f_left = (f + 15) % 16
    f_right = (f + 1) % 16

    barrier = pltpu.get_barrier_semaphore()
    for k in range(1, PLACES):
        pl.semaphore_signal(barrier, inc=1, device_id=((s + k) % PLACES, f), device_id_type=MESH_ID)
    for near in (f_left, f_right):
        pl.semaphore_signal(barrier, inc=1, device_id=(s, near), device_id_type=MESH_ID)
    pl.semaphore_wait(barrier, PLACES + 1)

    def cut_copy(k):
        p = (s + k) % PLACES
        if k == 0:
            return pltpu.make_async_copy(cutoffs.at[s], cut_all.at[s], cut_recv.at[0])
        return pltpu.make_async_remote_copy(
            src_ref=cutoffs.at[p],
            dst_ref=cut_all.at[s],
            send_sem=cut_send.at[k],
            recv_sem=cut_recv.at[k],
            device_id=(p, f),
            device_id_type=MESH_ID,
        )

    def in_copy(i, k):
        p = (s + k) % PLACES
        src = x.at[:, pl.ds(pl.multiple_of((p * CHUNKS + i) * GROUP, GROUP), GROUP), :]
        dst = inb.at[i, :, pl.ds(pl.multiple_of(s * GROUP, GROUP), GROUP), :]
        if k == 0:
            return pltpu.make_async_copy(src, dst, in_recv.at[i, 0])
        return pltpu.make_async_remote_copy(
            src_ref=src,
            dst_ref=dst,
            send_sem=in_send.at[i, k],
            recv_sem=in_recv.at[i, k],
            device_id=(p, f),
            device_id_type=MESH_ID,
        )

    def halo_copy(i, side):
        if side == 0:
            src, dst, near = inb.at[i, :, :, pl.ds(COLS - SIDE, SIDE)], left.at[i], f_right
        else:
            src, dst, near = inb.at[i, :, :, pl.ds(0, SIDE)], right.at[i], f_left
        return pltpu.make_async_remote_copy(
            src_ref=src,
            dst_ref=dst,
            send_sem=halo_send.at[i, side],
            recv_sem=halo_recv.at[i, side],
            device_id=(s, near),
            device_id_type=MESH_ID,
        )

    def out_copy(i, k):
        p = (s + k) % PLACES
        src = outb.at[i, :, pl.ds(pl.multiple_of(p * GROUP, GROUP), GROUP), :]
        dst = back.at[:, pl.ds(pl.multiple_of((s * CHUNKS + i) * GROUP, GROUP), GROUP), :]
        if k == 0:
            return pltpu.make_async_copy(src, dst, out_recv.at[i, 0])
        return pltpu.make_async_remote_copy(
            src_ref=src,
            dst_ref=dst,
            send_sem=out_send.at[i, k],
            recv_sem=out_recv.at[i, k],
            device_id=(p, f),
            device_id_type=MESH_ID,
        )

    def wait_arrival(copy, k):
        if k == 0:
            copy.wait()
        else:
            copy.wait_recv()

    order = (4, 3, 5, 2, 6, 1, 7, 0)
    for k in order:
        cut_copy(k).start()

    def start_in(i, carry):
        for k in order:
            in_copy(i, k).start()
        return carry

    lax.fori_loop(0, CHUNKS, start_in, 0)

    fill_rotations(angles, drive_bits, rot)
    fill_mixer(rot, mix_hi, mix_lo)
    fill_diagonal(f, diag)
    for k in range(PLACES):
        wait_arrival(cut_copy(k), k)

    def forward(i):
        for k in range(PLACES):
            wait_arrival(in_copy(i, k), k)
        halo_copy(i, 0).start()
        halo_copy(i, 1).start()

    for i in range(AHEAD):
        forward(i)

    def series_step(k, i, coef):
        link, low_side, high_side = coef
        source_re, source_im = (odd_re, odd_im) if k % 2 == 0 else (even_re, even_im)
        target_re, target_im = (even_re, even_im) if k % 2 == 0 else (odd_re, odd_im)
        start = HALO - k
        groups = -(-(OWN + 2 * k) // 4)

        def group(g, carry):
            n0 = start + 4 * g

            def tile(ref, j, t):
                return ref[pl.ds(pl.multiple_of((n0 + j) * 16 + t * 8, 8), 8), :]

            steps = [ladder[pl.ds(n0 + j, 8, stride=0), :] for j in range(5)]
            diagonal = [[tile(diag, j, t) for t in range(2)] for j in range(4)]
            for source, target, vec, sign, y in (
                (source_im, target_re, vec_re, 1, y_re),
                (source_re, target_im, vec_im, -1, y_im),
            ):
                p = [[tile(source, j, t) for t in range(2)] for j in range(-1, 5)]
                for j in range(4):
                    for t in range(2):
                        own = p[j + 1][t]
                        other = p[j + 1][1 - t]
                        far = pltpu.roll(other, 1 if t == 0 else 7, axis=0)
                        applied = (
                            diagonal[j][t] * own
                            + link * other
                            + (low_side if t == 0 else high_side) * far
                            + (steps[j] * p[j][t] + steps[j + 1] * p[j + 2][t])
                        )
                        if k == 0:
                            applied = 0.5 * applied
                        kept = OMEGA[k] * tile(vec, j, t)
                        if k < DEGREE - 1:
                            kept = kept + tile(target, j, t)
                        value = kept + applied if sign > 0 else kept - applied
                        if k == 0:
                            row = (n0 + j - HALO) * 16 + t
                            y[pl.ds(row, 8, stride=2), :] = value
                        else:
                            target[pl.ds(pl.multiple_of((n0 + j) * 16 + t * 8, 8), 8), :] = value
            return carry

        lax.fori_loop(0, groups, group, 0)

    def chunk(i, carry):
        @pl.when(i < CHUNKS - AHEAD)
        def _():
            forward(i + AHEAD)

        strength_first, strength_second = strengths(
            i, s, coupling_first, coupling_second, frozen_coupling, frozen_bits
        )
        cut = jnp.zeros((8, 128), jnp.int32)
        lane_place = iota((8, 128), 1) >> 4
        for q in range(PLACES):
            row = jnp.broadcast_to(cut_all[q], (8, 128))
            turned = pltpu.roll(row, ((q + 8 - i) * GROUP) % 128, axis=1)
            cut = jnp.where(lane_place == q, turned, cut)
        for block in range(9):
            level = f * OWN - HALO + block * 8 + iota((8, 128), 0)
            root = jnp.sqrt(jnp.maximum(level, 0).astype(jnp.float32) / FA)
            ladder[pl.ds(block * 8, 8), :] = jnp.where(
                (level >= 1) & (level < cut), 2.0 * strength_first * root, 0.0
            )
        sub = iota((8, 128), 0).astype(jnp.float32)
        double = 2.0 * strength_second
        link = double * jnp.sqrt((2.0 * sub + 1.0) / FB)
        low_side = double * jnp.sqrt(2.0 * sub / FB)
        high_side = jnp.where(sub < 7.0, double * jnp.sqrt((2.0 * sub + 2.0) / FB), 0.0)

        halo_copy(i, 0).wait_recv()
        halo_copy(i, 1).wait_recv()

        for part, natural in ((0, nat_re), (1, nat_im)):
            for b in range(8):
                if b < 2:
                    piece = left[i, part, :, b * 128 : (b + 1) * 128]
                elif b < 6:
                    piece = inb[i, part, :, (b - 2) * 128 : (b - 1) * 128]
                else:
                    piece = right[i, part, :, (b - 6) * 128 : (b - 5) * 128]
                natural[b * 128 : (b + 1) * 128, :] = piece.T

        def first_term(n, c):
            for natural, vec, even in ((nat_re, vec_re, even_re), (nat_im, vec_im, even_im)):
                for j in range(4):
                    for t in range(2):
                        value = natural[pl.ds((n * 4 + j) * 16 + t, 8, stride=2), :]
                        place = pl.ds(pl.multiple_of((n * 4 + j) * 16 + t * 8, 8), 8)
                        vec[place, :] = value
                        even[place, :] = OMEGA[DEGREE] * value
            return c

        lax.fori_loop(0, LEVELS // 4, first_term, 0)
        for k in range(DEGREE - 1, -1, -1):
            series_step(k, i, (link, low_side, high_side))

        y = jnp.concatenate([y_re[...], y_im[...]], axis=1)
        y_hi = y.astype(jnp.bfloat16)
        y_lo = (y - y_hi.astype(jnp.float32)).astype(jnp.bfloat16)

        def product(a, b):
            return lax.dot_general(
                a, b, (((1,), (1,)), ((), ())), preferred_element_type=jnp.float32
            )

        mixed = (
            product(mix_hi[...], y_hi) + product(mix_hi[...], y_lo) + product(mix_lo[...], y_hi)
        )
        outb[i, 0] = mixed[:LANES]
        outb[i, 1] = mixed[LANES:]
        for k in order:
            out_copy(i, k).start()
        return carry

    lax.fori_loop(0, CHUNKS, chunk, 0)

    def rotate_places(i, carry):
        for k in range(PLACES):
            wait_arrival(out_copy(i, k), k)

        def unit(u, c):
            half, col = u // 4, u % 4

            def spot(q):
                row = pl.multiple_of((q * CHUNKS + i) * GROUP + half * 8, 8)
                return pl.ds(row, 8), pl.ds(pl.multiple_of(col * 128, 128), 128)

            real = [back[0, spot(q)[0], spot(q)[1]] for q in range(PLACES)]
            imag = [back[1, spot(q)[0], spot(q)[1]] for q in range(PLACES)]
            real, imag = butterfly(real, imag, rot, (7, 8, 9))
            for q in range(PLACES):
                back[0, spot(q)[0], spot(q)[1]] = real[q]
                back[1, spot(q)[0], spot(q)[1]] = imag[q]
            return c

        lax.fori_loop(0, 8, unit, 0)
        return carry

    lax.fori_loop(0, CHUNKS, rotate_places, 0)

    def store_copy(q):
        rows = pl.ds(pl.multiple_of(q * 128, 128), 128)
        return pltpu.make_async_copy(back.at[:, rows, :], out.at[:, rows, :], store_sem.at[q])

    def rotate_chunks(q, carry):
        def unit(u, c):
            half, col = u // 4, u % 4

            def spot(i):
                row = pl.multiple_of((q * CHUNKS + i) * GROUP + half * 8, 8)
                return pl.ds(row, 8), pl.ds(pl.multiple_of(col * 128, 128), 128)

            real = [back[0, spot(i)[0], spot(i)[1]] for i in range(CHUNKS)]
            imag = [back[1, spot(i)[0], spot(i)[1]] for i in range(CHUNKS)]
            real, imag = butterfly(real, imag, rot, (4, 5, 6))
            for i in range(CHUNKS):
                back[0, spot(i)[0], spot(i)[1]] = real[i]
                back[1, spot(i)[0], spot(i)[1]] = imag[i]
            return c

        lax.fori_loop(0, 8, unit, 0)
        store_copy(q).start()
        return carry

    lax.fori_loop(0, PLACES, rotate_chunks, 0)

    def finish(i, carry):
        for k in range(1, PLACES):
            in_copy(i, k).wait_send()
            out_copy(i, k).wait_send()
        halo_copy(i, 0).wait_send()
        halo_copy(i, 1).wait_send()
        store_copy(i).wait()
        return carry

    lax.fori_loop(0, CHUNKS, finish, 0)
    for k in range(1, PLACES):
        cut_copy(k).wait_send()


def per_device(
    amplitudes,
    cutoffs,
    coupling_first,
    coupling_second,
    frozen_coupling,
    frozen_bits,
    drive_bits,
    angles,
):
    f32 = jnp.float32
    padded = pltpu.VMEM((PADDED * FB, LANES), f32)
    dma = pltpu.SemaphoreType.DMA
    smem = pl.BlockSpec(memory_space=pltpu.SMEM)
    return pl.pallas_call(
        kernel,
        name="evolve_and_rotate",
        out_shape=jax.ShapeDtypeStruct(amplitudes.shape, f32),
        in_specs=[
            pl.BlockSpec(memory_space=pl.ANY),
            pl.BlockSpec(memory_space=pltpu.VMEM),
            smem,
            smem,
            smem,
            smem,
            smem,
            smem,
        ],
        out_specs=pl.BlockSpec(memory_space=pl.ANY),
        scratch_shapes=[
            pltpu.VMEM((CHUNKS, 2, LANES, COLS), f32),
            pltpu.VMEM((PLACES, 1, 128), jnp.int32),
            pltpu.VMEM((CHUNKS, 2, LANES, SIDE), f32),
            pltpu.VMEM((CHUNKS, 2, LANES, SIDE), f32),
            pltpu.VMEM((LEVELS * FB, LANES), f32),
            pltpu.VMEM((LEVELS * FB, LANES), f32),
            padded,
            padded,
            padded,
            padded,
            padded,
            padded,
            pltpu.VMEM((COLS, LANES), f32),
            pltpu.VMEM((COLS, LANES), f32),
            padded,
            pltpu.VMEM((72, LANES), f32),
            pltpu.VMEM((3 * SPINS, 8, 128), f32),
            pltpu.VMEM((2 * LANES, 2 * LANES), jnp.bfloat16),
            pltpu.VMEM((2 * LANES, 2 * LANES), jnp.bfloat16),
            pltpu.VMEM((CHUNKS, 2, LANES, COLS), f32),
            pltpu.VMEM((2, CHUNKS * LANES, COLS), f32),
            dma((CHUNKS, PLACES)),
            dma((CHUNKS, PLACES)),
            dma((PLACES,)),
            dma((PLACES,)),
            dma((CHUNKS, 2)),
            dma((CHUNKS, 2)),
            dma((CHUNKS, PLACES)),
            dma((CHUNKS, PLACES)),
            dma((PLACES,)),
        ],
        compiler_params=pltpu.CompilerParams(
            collective_id=0, has_side_effects=True, vmem_limit_bytes=60 << 20
        ),
    )(
        amplitudes,
        cutoffs.reshape(PLACES, 1, 128),
        coupling_first,
        coupling_second,
        frozen_coupling,
        frozen_bits,
        drive_bits,
        angles,
    )


def solution(mesh):
    placed = (P(None, "spin", "fock"), P("spin"), P(), P(), P(), P(), P(), P())
    return jax.shard_map(
        per_device, mesh=mesh, in_specs=placed, out_specs=P(None, "spin", "fock"), check_vma=False
    )
```

```python
import math

import jax
import jax.numpy as jnp
from jax import lax
from jax.experimental import pallas as pl
from jax.experimental.pallas import tpu as pltpu
from jax.sharding import PartitionSpec as P

SPINS = 13
FA = 512
FB = 16
FROZEN = 16
DEGREE = 16
MESH_ID = pl.DeviceIdType.MESH

evolve_time = 12.0
diagonal_first = 0.06
diagonal_second = 0.04
ladder_first = 0.35
ladder_second = 0.1

PLACES = 8
CHUNKS = 8
GROUP = 16
LANES = PLACES * GROUP
OWN = 32
HALO = DEGREE
LEVELS = OWN + 2 * HALO
PADDED = LEVELS + 4
COLS = OWN * FB
SIDE = HALO * FB
LANE_BITS = (0, 1, 2, 3, 10, 11, 12)
AHEAD = 2


def bessel_first(term_order, argument):
    running = 0.0
    addend = (argument / 2.0) ** term_order / math.factorial(term_order)
    for serial in range(80):
        running = running + addend
        addend = addend * -(argument * argument / 4.0) / ((serial + 1) * (serial + 1 + term_order))
    return running


OMEGA = [(1.0 if k == 0 else 2.0) * bessel_first(k, evolve_time) for k in range(DEGREE + 1)]


def iota(shape, dim):
    return lax.broadcasted_iota(jnp.int32, shape, dim)


def fill_rotations(angles, drive_bits, rot):
    for j in range(SPINS):
        angle = jnp.full((8, 128), angles[j], jnp.float32)
        phase = jnp.full((8, 128), drive_bits[j], jnp.int32).astype(jnp.float32)
        sine = jnp.sin(angle)
        rot[3 * j] = jnp.cos(angle)
        rot[3 * j + 1] = sine * phase
        rot[3 * j + 2] = sine * (1.0 - phase)


def fill_mixer(rot, mix_hi, mix_lo):
    def rows(step, carry):
        base = pl.multiple_of(step * 16, 16)
        out_lane = base + iota((16, 128), 0)
        in_lane = iota((16, 128), 1)
        real = jnp.ones((16, 128), jnp.float32)
        imag = jnp.zeros((16, 128), jnp.float32)
        for place, bit in enumerate(LANE_BITS):
            out_bit = (out_lane >> place) & 1
            in_bit = (in_lane >> place) & 1
            same = out_bit == in_bit
            cosine = jnp.concatenate([rot[3 * bit]] * 2, axis=0)
            driven = jnp.concatenate([rot[3 * bit + 1]] * 2, axis=0)
            kept = jnp.concatenate([rot[3 * bit + 2]] * 2, axis=0)
            f_real = jnp.where(same, cosine, jnp.where(out_bit == 1, driven, -driven))
            f_imag = jnp.where(same, 0.0, -kept)
            real, imag = real * f_real - imag * f_imag, real * f_imag + imag * f_real
        top = jnp.concatenate([real, -imag], axis=1)
        low = jnp.concatenate([imag, real], axis=1)
        for start, value in ((0, top), (128, low)):
            high = value.astype(jnp.bfloat16)
            rest = (value - high.astype(jnp.float32)).astype(jnp.bfloat16)
            mix_hi[pl.ds(start + base, 16), :] = high
            mix_lo[pl.ds(start + base, 16), :] = rest
        return carry

    lax.fori_loop(0, 8, rows, 0)


def fill_diagonal(fock_place, diag):
    def rows(n, carry):
        row = iota((16, 128), 0)
        m = 2 * (row % 8) + row // 8
        level = fock_place * OWN - HALO + n
        level_float = jnp.full((16, 128), level, jnp.int32).astype(jnp.float32)
        value = diagonal_first * (2.0 * level_float / (FA - 1) - 1.0) + diagonal_second * (
            2.0 * m.astype(jnp.float32) / (FB - 1) - 1.0
        )
        diag[pl.ds(pl.multiple_of(n * 16, 16), 16), :] = 2.0 * value
        return carry

    lax.fori_loop(0, PADDED, rows, 0)


def strengths(chunk, spin_place, coupling_first, coupling_second, frozen_coupling, frozen_bits):
    shape = (8, 128)
    lane = iota(shape, 1)
    config = (lane >> 4) * 1024 + (spin_place * CHUNKS + chunk) * GROUP + (lane & 15)
    first = jnp.zeros(shape, jnp.float32)
    second = jnp.zeros(shape, jnp.float32)
    total_first = jnp.zeros(shape, jnp.float32)
    total_second = jnp.zeros(shape, jnp.float32)
    for j in range(SPINS):
        sign = (1 - 2 * ((config >> j) & 1)).astype(jnp.float32)
        first = first + coupling_first[j] * sign
        second = second + coupling_second[j] * sign
        total_first = total_first + coupling_first[j]
        total_second = total_second + coupling_second[j]
    for k in range(FROZEN):
        sign = jnp.full(shape, 1 - 2 * frozen_bits[k], jnp.int32).astype(jnp.float32)
        first = first + frozen_coupling[k] * sign
        total_first = total_first + frozen_coupling[k]
    return ladder_first * first / total_first, ladder_second * second / total_second


def butterfly(real, imag, bits):
    count = len(real)
    for place, (cosine, driven, kept) in bits:
        step = 1 << place
        for low in range(count):
            if low & step:
                continue
            up = low | step
            lr, li, ur, ui = real[low], imag[low], real[up], imag[up]
            real[low] = cosine * lr - driven * ur + kept * ui
            imag[low] = cosine * li - driven * ui - kept * ur
            real[up] = cosine * ur + driven * lr + kept * li
            imag[up] = cosine * ui + driven * li - kept * lr
    return real, imag


def kernel(
    x,
    cutoffs,
    coupling_first,
    coupling_second,
    frozen_coupling,
    frozen_bits,
    drive_bits,
    angles,
    back,
    rot_out,
    inb,
    cut_all,
    left,
    right,
    nat_re,
    nat_im,
    vec_re,
    vec_im,
    even_re,
    even_im,
    odd_re,
    odd_im,
    y_re,
    y_im,
    diag,
    ladder,
    rot,
    mix_hi,
    mix_lo,
    outb,
    in_send,
    in_recv,
    cut_send,
    cut_recv,
    halo_send,
    halo_recv,
    out_send,
    out_recv,
):
    s = lax.axis_index("spin")
    f = lax.axis_index("fock")
    f_left = (f + 15) % 16
    f_right = (f + 1) % 16

    barrier = pltpu.get_barrier_semaphore()
    for k in range(1, PLACES):
        pl.semaphore_signal(barrier, inc=1, device_id=((s + k) % PLACES, f), device_id_type=MESH_ID)
    for near in (f_left, f_right):
        pl.semaphore_signal(barrier, inc=1, device_id=(s, near), device_id_type=MESH_ID)
    pl.semaphore_wait(barrier, PLACES + 1)

    def cut_copy(k):
        p = (s + k) % PLACES
        if k == 0:
            return pltpu.make_async_copy(cutoffs.at[s], cut_all.at[s], cut_recv.at[0])
        return pltpu.make_async_remote_copy(
            src_ref=cutoffs.at[p],
            dst_ref=cut_all.at[s],
            send_sem=cut_send.at[k],
            recv_sem=cut_recv.at[k],
            device_id=(p, f),
            device_id_type=MESH_ID,
        )

    def in_copy(i, k):
        p = (s + k) % PLACES
        src = x.at[:, pl.ds(pl.multiple_of((p * CHUNKS + i) * GROUP, GROUP), GROUP), :]
        dst = inb.at[i, :, pl.ds(pl.multiple_of(s * GROUP, GROUP), GROUP), :]
        if k == 0:
            return pltpu.make_async_copy(src, dst, in_recv.at[i, 0])
        return pltpu.make_async_remote_copy(
            src_ref=src,
            dst_ref=dst,
            send_sem=in_send.at[i, k],
            recv_sem=in_recv.at[i, k],
            device_id=(p, f),
            device_id_type=MESH_ID,
        )

    def halo_copy(i, side):
        if side == 0:
            src, dst, near = inb.at[i, :, :, pl.ds(COLS - SIDE, SIDE)], left.at[i], f_right
        else:
            src, dst, near = inb.at[i, :, :, pl.ds(0, SIDE)], right.at[i], f_left
        return pltpu.make_async_remote_copy(
            src_ref=src,
            dst_ref=dst,
            send_sem=halo_send.at[i, side],
            recv_sem=halo_recv.at[i, side],
            device_id=(s, near),
            device_id_type=MESH_ID,
        )

    def out_copy(i, k):
        p = (s + k) % PLACES
        src = outb.at[i, :, pl.ds(pl.multiple_of(p * GROUP, GROUP), GROUP), :]
        dst = back.at[:, pl.ds(pl.multiple_of((s * CHUNKS + i) * GROUP, GROUP), GROUP), :]
        if k == 0:
            return pltpu.make_async_copy(src, dst, out_recv.at[i, 0])
        return pltpu.make_async_remote_copy(
            src_ref=src,
            dst_ref=dst,
            send_sem=out_send.at[i, k],
            recv_sem=out_recv.at[i, k],
            device_id=(p, f),
            device_id_type=MESH_ID,
        )

    def wait_arrival(copy, k):
        if k == 0:
            copy.wait()
        else:
            copy.wait_recv()

    order = (4, 3, 5, 2, 6, 1, 7, 0)
    for k in order:
        cut_copy(k).start()

    def start_in(i, carry):
        for k in order:
            in_copy(i, k).start()
        return carry

    lax.fori_loop(0, CHUNKS, start_in, 0)

    fill_rotations(angles, drive_bits, rot)
    fill_mixer(rot, mix_hi, mix_lo)
    fill_diagonal(f, diag)
    for k in range(PLACES):
        wait_arrival(cut_copy(k), k)

    def forward(i):
        for k in range(PLACES):
            wait_arrival(in_copy(i, k), k)
        halo_copy(i, 0).start()
        halo_copy(i, 1).start()

    for i in range(AHEAD):
        forward(i)

    def series_step(k, i, coef):
        link, low_side, high_side = coef
        source_re, source_im = (odd_re, odd_im) if k % 2 == 0 else (even_re, even_im)
        target_re, target_im = (even_re, even_im) if k % 2 == 0 else (odd_re, odd_im)
        start = HALO - k
        groups = -(-(OWN + 2 * k) // 4)

        def group(g, carry):
            n0 = start + 4 * g

            def tile(ref, j, t):
                return ref[pl.ds(pl.multiple_of((n0 + j) * 16 + t * 8, 8), 8), :]

            steps = [ladder[pl.ds(n0 + j, 8, stride=0), :] for j in range(5)]
            diagonal = [[tile(diag, j, t) for t in range(2)] for j in range(4)]
            for source, target, vec, sign, y in (
                (source_im, target_re, vec_re, 1, y_re),
                (source_re, target_im, vec_im, -1, y_im),
            ):
                p = [[tile(source, j, t) for t in range(2)] for j in range(-1, 5)]
                for j in range(4):
                    for t in range(2):
                        own = p[j + 1][t]
                        other = p[j + 1][1 - t]
                        far = pltpu.roll(other, 1 if t == 0 else 7, axis=0)
                        applied = (
                            diagonal[j][t] * own
                            + link * other
                            + (low_side if t == 0 else high_side) * far
                            + (steps[j] * p[j][t] + steps[j + 1] * p[j + 2][t])
                        )
                        if k == 0:
                            applied = 0.5 * applied
                        kept = OMEGA[k] * tile(vec, j, t)
                        if k < DEGREE - 1:
                            kept = kept + tile(target, j, t)
                        value = kept + applied if sign > 0 else kept - applied
                        if k == 0:
                            row = (n0 + j - HALO) * 16 + t
                            y[pl.ds(row, 8, stride=2), :] = value
                        else:
                            target[pl.ds(pl.multiple_of((n0 + j) * 16 + t * 8, 8), 8), :] = value
            return carry

        lax.fori_loop(0, groups, group, 0)

    def chunk(i, carry):
        strength_first, strength_second = strengths(
            i, s, coupling_first, coupling_second, frozen_coupling, frozen_bits
        )
        cut = jnp.zeros((8, 128), jnp.int32)
        lane_place = iota((8, 128), 1) >> 4
        for q in range(PLACES):
            row = jnp.broadcast_to(cut_all[q], (8, 128))
            turned = pltpu.roll(row, ((q + 8 - i) * GROUP) % 128, axis=1)
            cut = jnp.where(lane_place == q, turned, cut)
        for block in range(9):
            level = f * OWN - HALO + block * 8 + iota((8, 128), 0)
            root = jnp.sqrt(jnp.maximum(level, 0).astype(jnp.float32) / FA)
            ladder[pl.ds(block * 8, 8), :] = jnp.where(
                (level >= 1) & (level < cut), 2.0 * strength_first * root, 0.0
            )
        sub = iota((8, 128), 0).astype(jnp.float32)
        double = 2.0 * strength_second
        link = double * jnp.sqrt((2.0 * sub + 1.0) / FB)
        low_side = double * jnp.sqrt(2.0 * sub / FB)
        high_side = jnp.where(sub < 7.0, double * jnp.sqrt((2.0 * sub + 2.0) / FB), 0.0)

        halo_copy(i, 0).wait_recv()
        halo_copy(i, 1).wait_recv()

        for part, natural in ((0, nat_re), (1, nat_im)):
            for b in range(8):
                if b < 2:
                    piece = left[i, part, :, b * 128 : (b + 1) * 128]
                elif b < 6:
                    piece = inb[i, part, :, (b - 2) * 128 : (b - 1) * 128]
                else:
                    piece = right[i, part, :, (b - 6) * 128 : (b - 5) * 128]
                natural[b * 128 : (b + 1) * 128, :] = piece.T

        def first_term(n, c):
            for natural, vec, even in ((nat_re, vec_re, even_re), (nat_im, vec_im, even_im)):
                for j in range(4):
                    for t in range(2):
                        value = natural[pl.ds((n * 4 + j) * 16 + t, 8, stride=2), :]
                        place = pl.ds(pl.multiple_of((n * 4 + j) * 16 + t * 8, 8), 8)
                        vec[place, :] = value
                        even[place, :] = OMEGA[DEGREE] * value
            return c

        lax.fori_loop(0, LEVELS // 4, first_term, 0)
        for k in range(DEGREE - 1, -1, -1):
            series_step(k, i, (link, low_side, high_side))

        y = jnp.concatenate([y_re[...], y_im[...]], axis=1)
        y_hi = y.astype(jnp.bfloat16)
        y_lo = (y - y_hi.astype(jnp.float32)).astype(jnp.bfloat16)

        def product(a, b):
            return lax.dot_general(
                a, b, (((1,), (1,)), ((), ())), preferred_element_type=jnp.float32
            )

        mixed = (
            product(mix_hi[...], y_hi) + product(mix_hi[...], y_lo) + product(mix_lo[...], y_hi)
        )
        outb[i, 0] = mixed[:LANES]
        outb[i, 1] = mixed[LANES:]
        for k in order:
            out_copy(i, k).start()

        @pl.when(i < CHUNKS - AHEAD)
        def _():
            forward(i + AHEAD)

        return carry

    lax.fori_loop(0, CHUNKS, chunk, 0)

    def turn(bit):
        return rot[3 * bit], rot[3 * bit + 1], rot[3 * bit + 2]

    def rotate_places(i):
        for k in range(PLACES):
            wait_arrival(out_copy(i, k), k)

        def unit(u, c):
            half, col = u // 4, u % 4

            def spot(q):
                row = pl.multiple_of((q * CHUNKS + i) * GROUP + half * 8, 8)
                return pl.ds(row, 8), pl.ds(pl.multiple_of(col * 128, 128), 128)

            real = [back[0, spot(q)[0], spot(q)[1]] for q in range(PLACES)]
            imag = [back[1, spot(q)[0], spot(q)[1]] for q in range(PLACES)]
            turns = [(place, turn(7 + place)) for place in range(3)]
            real, imag = butterfly(real, imag, turns)
            for q in range(PLACES):
                back[0, spot(q)[0], spot(q)[1]] = real[q]
                back[1, spot(q)[0], spot(q)[1]] = imag[q]
            return c

        lax.fori_loop(0, 8, unit, 0)

    def rotate_pair(pair, carry):
        rotate_places(2 * pair)
        rotate_places(2 * pair + 1)

        def unit(u, c):
            q, col = u // 4, u % 4
            base = (q * CHUNKS + 2 * pair) * GROUP
            cols = pl.ds(pl.multiple_of(col * 128, 128), 128)
            for half in range(2):
                rows = [
                    pl.ds(pl.multiple_of(base + e * GROUP + half * 8, 8), 8) for e in range(2)
                ]
                real = [back[0, r, cols] for r in rows]
                imag = [back[1, r, cols] for r in rows]
                real, imag = butterfly(real, imag, [(0, turn(4))])
                for e in range(2):
                    back[0, rows[e], cols] = real[e]
                    back[1, rows[e], cols] = imag[e]
            return c

        lax.fori_loop(0, 4 * PLACES, unit, 0)
        return carry

    for j in range(6):
        rot_out[j] = rot[15 + j]
    lax.fori_loop(0, CHUNKS // 2, rotate_pair, 0)

    def finish(i, carry):
        for k in range(1, PLACES):
            in_copy(i, k).wait_send()
            out_copy(i, k).wait_send()
        halo_copy(i, 0).wait_send()
        halo_copy(i, 1).wait_send()
        return carry

    lax.fori_loop(0, CHUNKS, finish, 0)
    for k in range(1, PLACES):
        cut_copy(k).wait_send()


def last_kernel(back, rot, out, done, sems):
    def store_copy(q):
        rows = pl.ds(pl.multiple_of(q * 128, 128), 128)
        return pltpu.make_async_copy(done.at[:, rows, :], out.at[:, rows, :], sems.at[q])

    def rotate_chunks(q, carry):
        def unit(u, c):
            half, col = u // 4, u % 4

            def spot(i):
                row = pl.multiple_of((q * CHUNKS + i) * GROUP + half * 8, 8)
                return pl.ds(row, 8), pl.ds(pl.multiple_of(col * 128, 128), 128)

            real = [back[0, spot(i)[0], spot(i)[1]] for i in range(CHUNKS)]
            imag = [back[1, spot(i)[0], spot(i)[1]] for i in range(CHUNKS)]
            turns = [(1, (rot[0], rot[1], rot[2])), (2, (rot[3], rot[4], rot[5]))]
            real, imag = butterfly(real, imag, turns)
            for i in range(CHUNKS):
                done[0, spot(i)[0], spot(i)[1]] = real[i]
                done[1, spot(i)[0], spot(i)[1]] = imag[i]
            return c

        lax.fori_loop(0, 8, unit, 0)
        store_copy(q).start()
        return carry

    lax.fori_loop(0, PLACES, rotate_chunks, 0)

    def finish(q, carry):
        store_copy(q).wait()
        return carry

    lax.fori_loop(0, PLACES, finish, 0)


def per_device(
    amplitudes,
    cutoffs,
    coupling_first,
    coupling_second,
    frozen_coupling,
    frozen_bits,
    drive_bits,
    angles,
):
    f32 = jnp.float32
    padded = pltpu.VMEM((PADDED * FB, LANES), f32)
    dma = pltpu.SemaphoreType.DMA
    smem = pl.BlockSpec(memory_space=pltpu.SMEM)
    vmem = pl.BlockSpec(memory_space=pltpu.VMEM)
    back, rot = pl.pallas_call(
        kernel,
        name="evolve_and_rotate",
        out_shape=[
            pltpu.VMEM((2, CHUNKS * LANES, COLS), f32),
            pltpu.VMEM((6, 8, 128), f32),
        ],
        in_specs=[
            pl.BlockSpec(memory_space=pl.ANY),
            pl.BlockSpec(memory_space=pltpu.VMEM),
            smem,
            smem,
            smem,
            smem,
            smem,
            smem,
        ],
        out_specs=[vmem, vmem],
        scratch_shapes=[
            pltpu.VMEM((CHUNKS, 2, LANES, COLS), f32),
            pltpu.VMEM((PLACES, 1, 128), jnp.int32),
            pltpu.VMEM((CHUNKS, 2, LANES, SIDE), f32),
            pltpu.VMEM((CHUNKS, 2, LANES, SIDE), f32),
            pltpu.VMEM((LEVELS * FB, LANES), f32),
            pltpu.VMEM((LEVELS * FB, LANES), f32),
            padded,
            padded,
            padded,
            padded,
            padded,
            padded,
            pltpu.VMEM((COLS, LANES), f32),
            pltpu.VMEM((COLS, LANES), f32),
            padded,
            pltpu.VMEM((72, LANES), f32),
            pltpu.VMEM((3 * SPINS, 8, 128), f32),
            pltpu.VMEM((2 * LANES, 2 * LANES), jnp.bfloat16),
            pltpu.VMEM((2 * LANES, 2 * LANES), jnp.bfloat16),
            pltpu.VMEM((CHUNKS, 2, LANES, COLS), f32),
            dma((CHUNKS, PLACES)),
            dma((CHUNKS, PLACES)),
            dma((PLACES,)),
            dma((PLACES,)),
            dma((CHUNKS, 2)),
            dma((CHUNKS, 2)),
            dma((CHUNKS, PLACES)),
            dma((CHUNKS, PLACES)),
        ],
        compiler_params=pltpu.CompilerParams(
            collective_id=0, has_side_effects=True, vmem_limit_bytes=62_800_000
        ),
    )(
        amplitudes,
        cutoffs.reshape(PLACES, 1, 128),
        coupling_first,
        coupling_second,
        frozen_coupling,
        frozen_bits,
        drive_bits,
        angles,
    )
    return pl.pallas_call(
        last_kernel,
        name="rotate_last",
        out_shape=jax.ShapeDtypeStruct(amplitudes.shape, f32),
        in_specs=[vmem, vmem],
        out_specs=pl.BlockSpec(memory_space=pl.ANY),
        scratch_shapes=[pltpu.VMEM(amplitudes.shape, f32), dma((PLACES,))],
        compiler_params=pltpu.CompilerParams(vmem_limit_bytes=16 << 20),
    )(back, rot)


def solution(mesh):
    placed = (P(None, "spin", "fock"), P("spin"), P(), P(), P(), P(), P(), P())
    return jax.shard_map(
        per_device, mesh=mesh, in_specs=placed, out_specs=P(None, "spin", "fock"), check_vma=False
    )
```

```python
import math

import jax
import jax.numpy as jnp
from jax import lax
from jax.experimental import pallas as pl
from jax.experimental.pallas import tpu as pltpu
from jax.sharding import PartitionSpec as P

SPINS = 13
FA = 512
FB = 16
FROZEN = 16
DEGREE = 16
MESH_ID = pl.DeviceIdType.MESH

evolve_time = 12.0
diagonal_first = 0.06
diagonal_second = 0.04
ladder_first = 0.35
ladder_second = 0.1

PLACES = 8
CHUNKS = 8
GROUP = 16
LANES = PLACES * GROUP
OWN = 32
HALO = DEGREE
LEVELS = OWN + 2 * HALO
PADDED = LEVELS + 4
COLS = OWN * FB
SIDE = HALO * FB
LANE_BITS = (0, 1, 2, 3, 10, 11, 12)
AHEAD = 2
COL_TILES = COLS // 128
HALVES = GROUP // 8
LAST = CHUNKS - 1


def bessel_first(term_order, argument):
    running = 0.0
    addend = (argument / 2.0) ** term_order / math.factorial(term_order)
    for serial in range(80):
        running = running + addend
        addend = addend * -(argument * argument / 4.0) / ((serial + 1) * (serial + 1 + term_order))
    return running


OMEGA = [(1.0 if k == 0 else 2.0) * bessel_first(k, evolve_time) for k in range(DEGREE + 1)]


def iota(shape, dim):
    return lax.broadcasted_iota(jnp.int32, shape, dim)


def fill_rotations(angles, drive_bits, rot):
    for j in range(SPINS):
        angle = jnp.full((8, 128), angles[j], jnp.float32)
        phase = jnp.full((8, 128), drive_bits[j], jnp.int32).astype(jnp.float32)
        sine = jnp.sin(angle)
        rot[3 * j] = jnp.cos(angle)
        rot[3 * j + 1] = sine * phase
        rot[3 * j + 2] = sine * (1.0 - phase)


def fill_mixer(rot, mix_hi, mix_lo):
    def rows(step, carry):
        base = pl.multiple_of(step * 16, 16)
        out_lane = base + iota((16, 128), 0)
        in_lane = iota((16, 128), 1)
        real = jnp.ones((16, 128), jnp.float32)
        imag = jnp.zeros((16, 128), jnp.float32)
        for place, bit in enumerate(LANE_BITS):
            out_bit = (out_lane >> place) & 1
            in_bit = (in_lane >> place) & 1
            same = out_bit == in_bit
            cosine = jnp.concatenate([rot[3 * bit]] * 2, axis=0)
            driven = jnp.concatenate([rot[3 * bit + 1]] * 2, axis=0)
            kept = jnp.concatenate([rot[3 * bit + 2]] * 2, axis=0)
            f_real = jnp.where(same, cosine, jnp.where(out_bit == 1, driven, -driven))
            f_imag = jnp.where(same, 0.0, -kept)
            real, imag = real * f_real - imag * f_imag, real * f_imag + imag * f_real
        top = jnp.concatenate([real, -imag], axis=1)
        low = jnp.concatenate([imag, real], axis=1)
        for start, value in ((0, top), (128, low)):
            high = value.astype(jnp.bfloat16)
            rest = (value - high.astype(jnp.float32)).astype(jnp.bfloat16)
            mix_hi[pl.ds(start + base, 16), :] = high
            mix_lo[pl.ds(start + base, 16), :] = rest
        return carry

    lax.fori_loop(0, 8, rows, 0)


def fill_diagonal(fock_place, diag):
    def rows(n, carry):
        row = iota((16, 128), 0)
        m = 2 * (row % 8) + row // 8
        level = fock_place * OWN - HALO + n
        level_float = jnp.full((16, 128), level, jnp.int32).astype(jnp.float32)
        value = diagonal_first * (2.0 * level_float / (FA - 1) - 1.0) + diagonal_second * (
            2.0 * m.astype(jnp.float32) / (FB - 1) - 1.0
        )
        diag[pl.ds(pl.multiple_of(n * 16, 16), 16), :] = 2.0 * value
        return carry

    lax.fori_loop(0, PADDED, rows, 0)


def strengths(chunk, spin_place, coupling_first, coupling_second, frozen_coupling, frozen_bits):
    shape = (8, 128)
    lane = iota(shape, 1)
    config = (lane >> 4) * 1024 + (spin_place * CHUNKS + chunk) * GROUP + (lane & 15)
    first = jnp.zeros(shape, jnp.float32)
    second = jnp.zeros(shape, jnp.float32)
    total_first = jnp.zeros(shape, jnp.float32)
    total_second = jnp.zeros(shape, jnp.float32)
    for j in range(SPINS):
        sign = (1 - 2 * ((config >> j) & 1)).astype(jnp.float32)
        first = first + coupling_first[j] * sign
        second = second + coupling_second[j] * sign
        total_first = total_first + coupling_first[j]
        total_second = total_second + coupling_second[j]
    for k in range(FROZEN):
        sign = jnp.full(shape, 1 - 2 * frozen_bits[k], jnp.int32).astype(jnp.float32)
        first = first + frozen_coupling[k] * sign
        total_first = total_first + frozen_coupling[k]
    return ladder_first * first / total_first, ladder_second * second / total_second


def butterfly(real, imag, bits):
    count = len(real)
    for place, (cosine, driven, kept) in bits:
        step = 1 << place
        for low in range(count):
            if low & step:
                continue
            up = low | step
            lr, li, ur, ui = real[low], imag[low], real[up], imag[up]
            real[low] = cosine * lr - driven * ur + kept * ui
            imag[low] = cosine * li - driven * ui - kept * ur
            real[up] = cosine * ur + driven * lr + kept * li
            imag[up] = cosine * ui + driven * li - kept * lr
    return real, imag


def kernel(
    x,
    cutoffs,
    coupling_first,
    coupling_second,
    frozen_coupling,
    frozen_bits,
    drive_bits,
    angles,
    back,
    landed,
    coef_out,
    inb,
    cut_all,
    left,
    right,
    nat_re,
    nat_im,
    vec_re,
    vec_im,
    even_re,
    even_im,
    odd_re,
    odd_im,
    y_re,
    y_im,
    diag,
    ladder,
    rot,
    mix_hi,
    mix_lo,
    outb,
    in_send,
    in_recv,
    cut_send,
    cut_recv,
    halo_send,
    halo_recv,
    out_send,
    out_recv,
    tail_send,
    tail_recv,
):
    s = lax.axis_index("spin")
    f = lax.axis_index("fock")
    f_left = (f + 15) % 16
    f_right = (f + 1) % 16

    barrier = pltpu.get_barrier_semaphore()
    for k in range(1, PLACES):
        pl.semaphore_signal(barrier, inc=1, device_id=((s + k) % PLACES, f), device_id_type=MESH_ID)
    for near in (f_left, f_right):
        pl.semaphore_signal(barrier, inc=1, device_id=(s, near), device_id_type=MESH_ID)
    pl.semaphore_wait(barrier, PLACES + 1)

    def cut_copy(k):
        p = (s + k) % PLACES
        if k == 0:
            return pltpu.make_async_copy(cutoffs.at[s], cut_all.at[s], cut_recv.at[0])
        return pltpu.make_async_remote_copy(
            src_ref=cutoffs.at[p],
            dst_ref=cut_all.at[s],
            send_sem=cut_send.at[k],
            recv_sem=cut_recv.at[k],
            device_id=(p, f),
            device_id_type=MESH_ID,
        )

    def in_copy(i, k):
        p = (s + k) % PLACES
        src = x.at[:, pl.ds(pl.multiple_of((p * CHUNKS + i) * GROUP, GROUP), GROUP), :]
        dst = inb.at[i, :, pl.ds(pl.multiple_of(s * GROUP, GROUP), GROUP), :]
        if k == 0:
            return pltpu.make_async_copy(src, dst, in_recv.at[i, 0])
        return pltpu.make_async_remote_copy(
            src_ref=src,
            dst_ref=dst,
            send_sem=in_send.at[i, k],
            recv_sem=in_recv.at[i, k],
            device_id=(p, f),
            device_id_type=MESH_ID,
        )

    def halo_copy(i, side):
        if side == 0:
            src, dst, near = inb.at[i, :, :, pl.ds(COLS - SIDE, SIDE)], left.at[i], f_right
        else:
            src, dst, near = inb.at[i, :, :, pl.ds(0, SIDE)], right.at[i], f_left
        return pltpu.make_async_remote_copy(
            src_ref=src,
            dst_ref=dst,
            send_sem=halo_send.at[i, side],
            recv_sem=halo_recv.at[i, side],
            device_id=(s, near),
            device_id_type=MESH_ID,
        )

    def out_copy(i, k):
        p = (s + k) % PLACES
        src = outb.at[i, :, pl.ds(pl.multiple_of(p * GROUP, GROUP), GROUP), :]
        dst = back.at[:, s * CHUNKS + i]
        if k == 0:
            return pltpu.make_async_copy(src, dst, out_recv.at[i, 0])
        return pltpu.make_async_remote_copy(
            src_ref=src,
            dst_ref=dst,
            send_sem=out_send.at[i, k],
            recv_sem=out_recv.at[i, k],
            device_id=(p, f),
            device_id_type=MESH_ID,
        )

    def tail_copy(h, k):
        p = (s + k) % PLACES
        src = outb.at[LAST, :, pl.ds(pl.multiple_of(p * GROUP + h * 8, 8), 8), :]
        dst = landed.at[:, pl.ds(pl.multiple_of(s * GROUP + h * 8, 8), 8), :]
        if k == 0:
            return pltpu.make_async_copy(src, dst, tail_recv.at[h, 0])
        return pltpu.make_async_remote_copy(
            src_ref=src,
            dst_ref=dst,
            send_sem=tail_send.at[h, k],
            recv_sem=tail_recv.at[h, k],
            device_id=(p, f),
            device_id_type=MESH_ID,
        )

    def wait_arrival(copy, k):
        if k == 0:
            copy.wait()
        else:
            copy.wait_recv()

    order = (4, 3, 5, 2, 6, 1, 7, 0)
    for k in order:
        cut_copy(k).start()

    def start_in(i, carry):
        for k in order:
            in_copy(i, k).start()
        return carry

    lax.fori_loop(0, CHUNKS, start_in, 0)

    fill_rotations(angles, drive_bits, rot)
    fill_mixer(rot, mix_hi, mix_lo)
    fill_diagonal(f, diag)
    for k in range(PLACES):
        wait_arrival(cut_copy(k), k)

    def forward(i):
        for k in range(PLACES):
            wait_arrival(in_copy(i, k), k)
        halo_copy(i, 0).start()
        halo_copy(i, 1).start()

    for i in range(AHEAD):
        forward(i)

    def series_step(k, i, coef):
        link, low_side, high_side = coef
        source_re, source_im = (odd_re, odd_im) if k % 2 == 0 else (even_re, even_im)
        target_re, target_im = (even_re, even_im) if k % 2 == 0 else (odd_re, odd_im)
        start = HALO - k
        groups = -(-(OWN + 2 * k) // 4)

        def group(g, carry):
            n0 = start + 4 * g

            def tile(ref, j, t):
                return ref[pl.ds(pl.multiple_of((n0 + j) * 16 + t * 8, 8), 8), :]

            steps = [ladder[pl.ds(n0 + j, 8, stride=0), :] for j in range(5)]
            diagonal = [[tile(diag, j, t) for t in range(2)] for j in range(4)]
            for source, target, vec, sign, y in (
                (source_im, target_re, vec_re, 1, y_re),
                (source_re, target_im, vec_im, -1, y_im),
            ):
                p = [[tile(source, j, t) for t in range(2)] for j in range(-1, 5)]
                for j in range(4):
                    for t in range(2):
                        own = p[j + 1][t]
                        other = p[j + 1][1 - t]
                        far = pltpu.roll(other, 1 if t == 0 else 7, axis=0)
                        applied = (
                            diagonal[j][t] * own
                            + link * other
                            + (low_side if t == 0 else high_side) * far
                            + (steps[j] * p[j][t] + steps[j + 1] * p[j + 2][t])
                        )
                        if k == 0:
                            applied = 0.5 * applied
                        kept = OMEGA[k] * tile(vec, j, t)
                        if k < DEGREE - 1:
                            kept = kept + tile(target, j, t)
                        value = kept + applied if sign > 0 else kept - applied
                        if k == 0:
                            row = (n0 + j - HALO) * 16 + t
                            y[pl.ds(row, 8, stride=2), :] = value
                        else:
                            target[pl.ds(pl.multiple_of((n0 + j) * 16 + t * 8, 8), 8), :] = value
            return carry

        lax.fori_loop(0, groups, group, 0)

    def chunk(i, carry):
        strength_first, strength_second = strengths(
            i, s, coupling_first, coupling_second, frozen_coupling, frozen_bits
        )
        cut = jnp.zeros((8, 128), jnp.int32)
        lane_place = iota((8, 128), 1) >> 4
        for q in range(PLACES):
            row = jnp.broadcast_to(cut_all[q], (8, 128))
            turned = pltpu.roll(row, ((q + 8 - i) * GROUP) % 128, axis=1)
            cut = jnp.where(lane_place == q, turned, cut)
        for block in range(9):
            level = f * OWN - HALO + block * 8 + iota((8, 128), 0)
            root = jnp.sqrt(jnp.maximum(level, 0).astype(jnp.float32) / FA)
            ladder[pl.ds(block * 8, 8), :] = jnp.where(
                (level >= 1) & (level < cut), 2.0 * strength_first * root, 0.0
            )
        sub = iota((8, 128), 0).astype(jnp.float32)
        double = 2.0 * strength_second
        link = double * jnp.sqrt((2.0 * sub + 1.0) / FB)
        low_side = double * jnp.sqrt(2.0 * sub / FB)
        high_side = jnp.where(sub < 7.0, double * jnp.sqrt((2.0 * sub + 2.0) / FB), 0.0)

        halo_copy(i, 0).wait_recv()
        halo_copy(i, 1).wait_recv()

        for part, natural in ((0, nat_re), (1, nat_im)):
            for b in range(8):
                if b < 2:
                    piece = left[i, part, :, b * 128 : (b + 1) * 128]
                elif b < 6:
                    piece = inb[i, part, :, (b - 2) * 128 : (b - 1) * 128]
                else:
                    piece = right[i, part, :, (b - 6) * 128 : (b - 5) * 128]
                natural[b * 128 : (b + 1) * 128, :] = piece.T

        def first_term(n, c):
            for natural, vec, even in ((nat_re, vec_re, even_re), (nat_im, vec_im, even_im)):
                for j in range(4):
                    for t in range(2):
                        value = natural[pl.ds((n * 4 + j) * 16 + t, 8, stride=2), :]
                        place = pl.ds(pl.multiple_of((n * 4 + j) * 16 + t * 8, 8), 8)
                        vec[place, :] = value
                        even[place, :] = OMEGA[DEGREE] * value
            return c

        lax.fori_loop(0, LEVELS // 4, first_term, 0)
        for k in range(DEGREE - 1, -1, -1):
            series_step(k, i, (link, low_side, high_side))

        y = jnp.concatenate([y_re[...], y_im[...]], axis=1)
        y_hi = y.astype(jnp.bfloat16)
        y_lo = (y - y_hi.astype(jnp.float32)).astype(jnp.bfloat16)

        def product(a, b):
            return lax.dot_general(
                a, b, (((1,), (1,)), ((), ())), preferred_element_type=jnp.float32
            )

        mixed = (
            product(mix_hi[...], y_hi) + product(mix_hi[...], y_lo) + product(mix_lo[...], y_hi)
        )
        outb[i, 0] = mixed[:LANES]
        outb[i, 1] = mixed[LANES:]

        @pl.when(i < LAST)
        def _():
            for k in order:
                out_copy(i, k).start()

        @pl.when(i == LAST)
        def _():
            for h in range(HALVES):
                for k in order:
                    tail_copy(h, k).start()

        @pl.when(i < CHUNKS - AHEAD)
        def _():
            forward(i + AHEAD)

        return carry

    lax.fori_loop(0, CHUNKS, chunk, 0)

    def turn(bit):
        return rot[3 * bit], rot[3 * bit + 1], rot[3 * bit + 2]

    for place in range(9):
        coef_out[2 * CHUNKS + place] = rot[21 + place]
    for i in range(CHUNKS):
        real = jnp.ones((8, 128), jnp.float32)
        imag = jnp.zeros((8, 128), jnp.float32)
        for place in range(3):
            cosine, driven, kept = turn(4 + place)
            if (i >> place) & 1:
                real, imag = real * cosine, imag * cosine
            else:
                real, imag = imag * kept - real * driven, -real * kept - imag * driven
        coef_out[i] = real
        coef_out[CHUNKS + i] = imag

    def spot(q, i, half, col):
        return (
            q * CHUNKS + i,
            pl.ds(pl.multiple_of(half * 8, 8), 8),
            pl.ds(pl.multiple_of(col * 128, 128), 128),
        )

    def rotate_places(i, carry):
        for k in range(PLACES):
            wait_arrival(out_copy(i, k), k)

        def unit(u, c):
            half, col = u // COL_TILES, u % COL_TILES
            spots = [spot(q, i, half, col) for q in range(PLACES)]
            real = [back[0, g, r, l] for g, r, l in spots]
            imag = [back[1, g, r, l] for g, r, l in spots]
            real, imag = butterfly(real, imag, [(place, turn(7 + place)) for place in range(3)])
            for q, (g, r, l) in enumerate(spots):
                back[0, g, r, l] = real[q]
                back[1, g, r, l] = imag[q]
            return c

        lax.fori_loop(0, 2 * COL_TILES, unit, 0)
        return carry

    lax.fori_loop(0, LAST, rotate_places, 0)

    def rotate_chunks(q, carry):
        def unit(u, c):
            half, col = u // COL_TILES, u % COL_TILES
            spots = [spot(q, i, half, col) for i in range(CHUNKS)]
            zero = jnp.zeros((8, 128), jnp.float32)
            real = [back[0, g, r, l] for g, r, l in spots[:LAST]] + [zero]
            imag = [back[1, g, r, l] for g, r, l in spots[:LAST]] + [zero]
            real, imag = butterfly(real, imag, [(place, turn(4 + place)) for place in range(3)])
            for i, (g, r, l) in enumerate(spots):
                back[0, g, r, l] = real[i]
                back[1, g, r, l] = imag[i]
            return c

        lax.fori_loop(0, 2 * COL_TILES, unit, 0)
        return carry

    lax.fori_loop(0, PLACES, rotate_chunks, 0)

    def drain(i, carry):
        for k in range(1, PLACES):
            in_copy(i, k).wait_send()
        halo_copy(i, 0).wait_send()
        halo_copy(i, 1).wait_send()

        @pl.when(i < LAST)
        def _():
            for k in range(1, PLACES):
                out_copy(i, k).wait_send()

        return carry

    lax.fori_loop(0, CHUNKS, drain, 0)
    for k in range(1, PLACES):
        cut_copy(k).wait_send()

    for h in range(HALVES):
        for k in range(PLACES):
            wait_arrival(tail_copy(h, k), k)
        if h < HALVES - 1:

            def finish(col, carry):
                finish_tile(landed, back, back, coef_out, h, h, col)
                return carry

            lax.fori_loop(0, COL_TILES, finish, 0)
    for h in range(HALVES):
        for k in range(1, PLACES):
            tail_copy(h, k).wait_send()


def finish_tile(landed, partial, done, coef, half, target, col):
    cols = pl.ds(pl.multiple_of(col * 128, 128), 128)
    rows = [pl.ds(q * GROUP + half * 8, 8) for q in range(PLACES)]
    real = [landed[0, r, cols] for r in rows]
    imag = [landed[1, r, cols] for r in rows]
    base = 2 * CHUNKS
    turns = [(place, tuple(coef[base + 3 * place + e] for e in range(3))) for place in range(3)]
    real, imag = butterfly(real, imag, turns)
    source, place = pl.ds(half * 8, 8), pl.ds(target * 8, 8)
    for i in range(CHUNKS):
        k_real, k_imag = coef[i], coef[CHUNKS + i]
        for q in range(PLACES):
            g = q * CHUNKS + i
            new_real = partial[0, g, source, cols] + (k_real * real[q] - k_imag * imag[q])
            new_imag = partial[1, g, source, cols] + (k_real * imag[q] + k_imag * real[q])
            done[0, g, place, cols] = new_real
            done[1, g, place, cols] = new_imag


def last_kernel(back, landed, coef, out, done, ready_sems, sems):
    ready = (HALVES - 1) * 8
    parts = []
    for j in range(4):
        groups = pl.ds(j * 16, 16)
        parts.append(
            pltpu.make_async_copy(
                back.at[:, groups, pl.ds(0, ready), :],
                out.at[:, groups, pl.ds(0, ready), :],
                ready_sems.at[j],
            )
        )
    for part in parts:
        part.start()

    def store_copy(col):
        cols = pl.ds(pl.multiple_of(col * 128, 128), 128)
        return pltpu.make_async_copy(
            done.at[:, :, :, cols], out.at[:, :, pl.ds(ready, 8), cols], sems.at[col]
        )

    def finish(col, carry):
        finish_tile(landed, back, done, coef, HALVES - 1, 0, col)
        store_copy(col).start()
        return carry

    lax.fori_loop(0, COL_TILES, finish, 0)
    for part in parts:
        part.wait()
    for col in range(COL_TILES):
        store_copy(col).wait()


def per_device(
    amplitudes,
    cutoffs,
    coupling_first,
    coupling_second,
    frozen_coupling,
    frozen_bits,
    drive_bits,
    angles,
):
    f32 = jnp.float32
    padded = pltpu.VMEM((PADDED * FB, LANES), f32)
    dma = pltpu.SemaphoreType.DMA
    smem = pl.BlockSpec(memory_space=pltpu.SMEM)
    vmem = pl.BlockSpec(memory_space=pltpu.VMEM)
    back, landed, coef = pl.pallas_call(
        kernel,
        name="evolve_and_rotate",
        out_shape=[
            pltpu.VMEM((2, PLACES * CHUNKS, GROUP, COLS), f32),
            pltpu.VMEM((2, LANES, COLS), f32),
            pltpu.VMEM((2 * CHUNKS + 9, 8, 128), f32),
        ],
        in_specs=[
            pl.BlockSpec(memory_space=pl.ANY),
            pl.BlockSpec(memory_space=pltpu.VMEM),
            smem,
            smem,
            smem,
            smem,
            smem,
            smem,
        ],
        out_specs=[vmem, vmem, vmem],
        scratch_shapes=[
            pltpu.VMEM((CHUNKS, 2, LANES, COLS), f32),
            pltpu.VMEM((PLACES, 1, 128), jnp.int32),
            pltpu.VMEM((CHUNKS, 2, LANES, SIDE), f32),
            pltpu.VMEM((CHUNKS, 2, LANES, SIDE), f32),
            pltpu.VMEM((LEVELS * FB, LANES), f32),
            pltpu.VMEM((LEVELS * FB, LANES), f32),
            padded,
            padded,
            padded,
            padded,
            padded,
            padded,
            pltpu.VMEM((COLS, LANES), f32),
            pltpu.VMEM((COLS, LANES), f32),
            padded,
            pltpu.VMEM((72, LANES), f32),
            pltpu.VMEM((3 * SPINS, 8, 128), f32),
            pltpu.VMEM((2 * LANES, 2 * LANES), jnp.bfloat16),
            pltpu.VMEM((2 * LANES, 2 * LANES), jnp.bfloat16),
            pltpu.VMEM((CHUNKS, 2, LANES, COLS), f32),
            dma((CHUNKS, PLACES)),
            dma((CHUNKS, PLACES)),
            dma((PLACES,)),
            dma((PLACES,)),
            dma((CHUNKS, 2)),
            dma((CHUNKS, 2)),
            dma((CHUNKS, PLACES)),
            dma((CHUNKS, PLACES)),
            dma((HALVES, PLACES)),
            dma((HALVES, PLACES)),
        ],
        compiler_params=pltpu.CompilerParams(
            collective_id=0, has_side_effects=True, vmem_limit_bytes=62_000_000
        ),
    )(
        amplitudes,
        cutoffs.reshape(PLACES, 1, 128),
        coupling_first,
        coupling_second,
        frozen_coupling,
        frozen_bits,
        drive_bits,
        angles,
    )
    rotated = pl.pallas_call(
        last_kernel,
        name="rotate_last",
        out_shape=jax.ShapeDtypeStruct((2, PLACES * CHUNKS, GROUP, COLS), f32),
        in_specs=[vmem, vmem, vmem],
        out_specs=pl.BlockSpec(memory_space=pl.ANY),
        scratch_shapes=[
            pltpu.VMEM((2, PLACES * CHUNKS, 8, COLS), f32),
            dma((4,)),
            dma((COL_TILES,)),
        ],
        compiler_params=pltpu.CompilerParams(vmem_limit_bytes=16 << 20),
    )(back, landed, coef)
    return rotated.reshape(amplitudes.shape)


def solution(mesh):
    placed = (P(None, "spin", "fock"), P("spin"), P(), P(), P(), P(), P(), P())
    return jax.shard_map(
        per_device, mesh=mesh, in_specs=placed, out_specs=P(None, "spin", "fock"), check_vma=False
    )
```

```python
import math

import jax
import jax.numpy as jnp
from jax import lax
from jax.experimental import pallas as pl
from jax.experimental.pallas import tpu as pltpu
from jax.sharding import PartitionSpec as P

SPINS = 13
FA = 512
FB = 16
FROZEN = 16
DEGREE = 16
MESH_ID = pl.DeviceIdType.MESH

evolve_time = 12.0
diagonal_first = 0.06
diagonal_second = 0.04
ladder_first = 0.35
ladder_second = 0.1

PLACES = 8
CHUNKS = 8
GROUP = 16
LANES = PLACES * GROUP
OWN = 32
HALO = DEGREE
LEVELS = OWN + 2 * HALO
PADDED = LEVELS + 4
COLS = OWN * FB
SIDE = HALO * FB
LANE_BITS = (0, 1, 2, 3, 10, 11, 12)
AHEAD = 2
COL_TILES = COLS // 128
HALVES = GROUP // 8
LAST = CHUNKS - 1


def bessel_first(term_order, argument):
    running = 0.0
    addend = (argument / 2.0) ** term_order / math.factorial(term_order)
    for serial in range(80):
        running = running + addend
        addend = addend * -(argument * argument / 4.0) / ((serial + 1) * (serial + 1 + term_order))
    return running


OMEGA = [(1.0 if k == 0 else 2.0) * bessel_first(k, evolve_time) for k in range(DEGREE + 1)]


def iota(shape, dim):
    return lax.broadcasted_iota(jnp.int32, shape, dim)


def fill_rotations(angles, drive_bits, rot):
    for j in range(SPINS):
        angle = jnp.full((8, 128), angles[j], jnp.float32)
        phase = jnp.full((8, 128), drive_bits[j], jnp.int32).astype(jnp.float32)
        sine = jnp.sin(angle)
        rot[3 * j] = jnp.cos(angle)
        rot[3 * j + 1] = sine * phase
        rot[3 * j + 2] = sine * (1.0 - phase)


def fill_mixer(rot, mix_hi, mix_lo):
    def rows(step, carry):
        base = pl.multiple_of(step * 16, 16)
        out_lane = base + iota((16, 128), 0)
        in_lane = iota((16, 128), 1)
        real = jnp.ones((16, 128), jnp.float32)
        imag = jnp.zeros((16, 128), jnp.float32)
        for place, bit in enumerate(LANE_BITS):
            out_bit = (out_lane >> place) & 1
            in_bit = (in_lane >> place) & 1
            same = out_bit == in_bit
            cosine = jnp.concatenate([rot[3 * bit]] * 2, axis=0)
            driven = jnp.concatenate([rot[3 * bit + 1]] * 2, axis=0)
            kept = jnp.concatenate([rot[3 * bit + 2]] * 2, axis=0)
            f_real = jnp.where(same, cosine, jnp.where(out_bit == 1, driven, -driven))
            f_imag = jnp.where(same, 0.0, -kept)
            real, imag = real * f_real - imag * f_imag, real * f_imag + imag * f_real
        top = jnp.concatenate([real, -imag], axis=1)
        low = jnp.concatenate([imag, real], axis=1)
        for start, value in ((0, top), (128, low)):
            high = value.astype(jnp.bfloat16)
            rest = (value - high.astype(jnp.float32)).astype(jnp.bfloat16)
            mix_hi[pl.ds(start + base, 16), :] = high
            mix_lo[pl.ds(start + base, 16), :] = rest
        return carry

    lax.fori_loop(0, 8, rows, 0)


def fill_diagonal(fock_place, diag):
    def rows(n, carry):
        row = iota((16, 128), 0)
        m = 2 * (row % 8) + row // 8
        level = fock_place * OWN - HALO + n
        level_float = jnp.full((16, 128), level, jnp.int32).astype(jnp.float32)
        value = diagonal_first * (2.0 * level_float / (FA - 1) - 1.0) + diagonal_second * (
            2.0 * m.astype(jnp.float32) / (FB - 1) - 1.0
        )
        diag[pl.ds(pl.multiple_of(n * 16, 16), 16), :] = 2.0 * value
        return carry

    lax.fori_loop(0, PADDED, rows, 0)


def strengths(chunk, spin_place, coupling_first, coupling_second, frozen_coupling, frozen_bits):
    shape = (8, 128)
    lane = iota(shape, 1)
    config = (lane >> 4) * 1024 + (spin_place * CHUNKS + chunk) * GROUP + (lane & 15)
    first = jnp.zeros(shape, jnp.float32)
    second = jnp.zeros(shape, jnp.float32)
    total_first = jnp.zeros(shape, jnp.float32)
    total_second = jnp.zeros(shape, jnp.float32)
    for j in range(SPINS):
        sign = (1 - 2 * ((config >> j) & 1)).astype(jnp.float32)
        first = first + coupling_first[j] * sign
        second = second + coupling_second[j] * sign
        total_first = total_first + coupling_first[j]
        total_second = total_second + coupling_second[j]
    for k in range(FROZEN):
        sign = jnp.full(shape, 1 - 2 * frozen_bits[k], jnp.int32).astype(jnp.float32)
        first = first + frozen_coupling[k] * sign
        total_first = total_first + frozen_coupling[k]
    return ladder_first * first / total_first, ladder_second * second / total_second


def butterfly(real, imag, bits):
    count = len(real)
    for place, (cosine, driven, kept) in bits:
        step = 1 << place
        for low in range(count):
            if low & step:
                continue
            up = low | step
            lr, li, ur, ui = real[low], imag[low], real[up], imag[up]
            real[low] = cosine * lr - driven * ur + kept * ui
            imag[low] = cosine * li - driven * ui - kept * ur
            real[up] = cosine * ur + driven * lr + kept * li
            imag[up] = cosine * ui + driven * li - kept * lr
    return real, imag


def kernel(
    x,
    cutoffs,
    coupling_first,
    coupling_second,
    frozen_coupling,
    frozen_bits,
    drive_bits,
    angles,
    back,
    landed,
    coef_out,
    inb,
    cut_all,
    left,
    right,
    nat_re,
    nat_im,
    vec_re,
    vec_im,
    even_re,
    even_im,
    odd_re,
    odd_im,
    y_re,
    y_im,
    diag,
    ladder,
    rot,
    mix_hi,
    mix_lo,
    outb,
    in_send,
    in_recv,
    cut_send,
    cut_recv,
    halo_send,
    halo_recv,
    out_send,
    out_recv,
    tail_send,
    tail_recv,
):
    s = lax.axis_index("spin")
    f = lax.axis_index("fock")
    f_left = (f + 15) % 16
    f_right = (f + 1) % 16

    barrier = pltpu.get_barrier_semaphore()
    for k in range(1, PLACES):
        pl.semaphore_signal(barrier, inc=1, device_id=((s + k) % PLACES, f), device_id_type=MESH_ID)
    for near in (f_left, f_right):
        pl.semaphore_signal(barrier, inc=1, device_id=(s, near), device_id_type=MESH_ID)
    pl.semaphore_wait(barrier, PLACES + 1)

    def cut_copy(k):
        p = (s + k) % PLACES
        if k == 0:
            return pltpu.make_async_copy(cutoffs.at[s], cut_all.at[s], cut_recv)
        return pltpu.make_async_remote_copy(
            src_ref=cutoffs.at[p],
            dst_ref=cut_all.at[s],
            send_sem=cut_send,
            recv_sem=cut_recv,
            device_id=(p, f),
            device_id_type=MESH_ID,
        )

    def in_copy(i, k):
        p = (s + k) % PLACES
        src = x.at[:, pl.ds(pl.multiple_of((p * CHUNKS + i) * GROUP, GROUP), GROUP), :]
        dst = inb.at[i, :, pl.ds(pl.multiple_of(s * GROUP, GROUP), GROUP), :]
        if k == 0:
            return pltpu.make_async_copy(src, dst, in_recv.at[i])
        return pltpu.make_async_remote_copy(
            src_ref=src,
            dst_ref=dst,
            send_sem=in_send,
            recv_sem=in_recv.at[i],
            device_id=(p, f),
            device_id_type=MESH_ID,
        )

    def halo_copy(i, side):
        if side == 0:
            src, dst, near = inb.at[i, :, :, pl.ds(COLS - SIDE, SIDE)], left.at[i], f_right
        else:
            src, dst, near = inb.at[i, :, :, pl.ds(0, SIDE)], right.at[i], f_left
        return pltpu.make_async_remote_copy(
            src_ref=src,
            dst_ref=dst,
            send_sem=halo_send,
            recv_sem=halo_recv.at[i],
            device_id=(s, near),
            device_id_type=MESH_ID,
        )

    def out_copy(i, k):
        p = (s + k) % PLACES
        src = outb.at[i, :, pl.ds(pl.multiple_of(p * GROUP, GROUP), GROUP), :]
        dst = back.at[:, s * CHUNKS + i]
        if k == 0:
            return pltpu.make_async_copy(src, dst, out_recv.at[i])
        return pltpu.make_async_remote_copy(
            src_ref=src,
            dst_ref=dst,
            send_sem=out_send,
            recv_sem=out_recv.at[i],
            device_id=(p, f),
            device_id_type=MESH_ID,
        )

    def tail_copy(h, k):
        p = (s + k) % PLACES
        src = outb.at[LAST, :, pl.ds(pl.multiple_of(p * GROUP + h * 8, 8), 8), :]
        dst = landed.at[:, pl.ds(pl.multiple_of(s * GROUP + h * 8, 8), 8), :]
        if k == 0:
            return pltpu.make_async_copy(src, dst, tail_recv.at[h])
        return pltpu.make_async_remote_copy(
            src_ref=src,
            dst_ref=dst,
            send_sem=tail_send,
            recv_sem=tail_recv.at[h],
            device_id=(p, f),
            device_id_type=MESH_ID,
        )

    def wait_for(sem, like):
        pltpu.make_async_copy(like, like, sem).wait()

    others = pl.ds(0, LANES - GROUP)

    order = (4, 3, 5, 2, 6, 1, 7, 0)
    for k in order:
        cut_copy(k).start()

    def start_in(i, carry):
        for k in order:
            in_copy(i, k).start()
        return carry

    lax.fori_loop(0, CHUNKS, start_in, 0)

    fill_rotations(angles, drive_bits, rot)
    fill_mixer(rot, mix_hi, mix_lo)
    fill_diagonal(f, diag)
    wait_for(cut_recv, cut_all)

    def forward(i):
        wait_for(in_recv.at[i], inb.at[i])
        halo_copy(i, 0).start()
        halo_copy(i, 1).start()

    for i in range(AHEAD):
        forward(i)

    def series_step(k, i, coef):
        link, low_side, high_side = coef
        source_re, source_im = (odd_re, odd_im) if k % 2 == 0 else (even_re, even_im)
        target_re, target_im = (even_re, even_im) if k % 2 == 0 else (odd_re, odd_im)
        start = HALO - k
        groups = -(-(OWN + 2 * k) // 4)

        def group(g, carry):
            n0 = start + 4 * g

            def tile(ref, j, t):
                return ref[pl.ds(pl.multiple_of((n0 + j) * 16 + t * 8, 8), 8), :]

            steps = [ladder[pl.ds(n0 + j, 8, stride=0), :] for j in range(5)]
            diagonal = [[tile(diag, j, t) for t in range(2)] for j in range(4)]
            for source, target, vec, sign, y in (
                (source_im, target_re, vec_re, 1, y_re),
                (source_re, target_im, vec_im, -1, y_im),
            ):
                p = [[tile(source, j, t) for t in range(2)] for j in range(-1, 5)]
                for j in range(4):
                    for t in range(2):
                        own = p[j + 1][t]
                        other = p[j + 1][1 - t]
                        far = pltpu.roll(other, 1 if t == 0 else 7, axis=0)
                        applied = (
                            diagonal[j][t] * own
                            + link * other
                            + (low_side if t == 0 else high_side) * far
                            + (steps[j] * p[j][t] + steps[j + 1] * p[j + 2][t])
                        )
                        if k == 0:
                            applied = 0.5 * applied
                        kept = OMEGA[k] * tile(vec, j, t)
                        if k < DEGREE - 1:
                            kept = kept + tile(target, j, t)
                        value = kept + applied if sign > 0 else kept - applied
                        if k == 0:
                            row = (n0 + j - HALO) * 16 + t
                            y[pl.ds(row, 8, stride=2), :] = value
                        else:
                            target[pl.ds(pl.multiple_of((n0 + j) * 16 + t * 8, 8), 8), :] = value
            return carry

        lax.fori_loop(0, groups, group, 0)

    def chunk(i, carry):
        strength_first, strength_second = strengths(
            i, s, coupling_first, coupling_second, frozen_coupling, frozen_bits
        )
        cut = jnp.zeros((8, 128), jnp.int32)
        lane_place = iota((8, 128), 1) >> 4
        for q in range(PLACES):
            row = jnp.broadcast_to(cut_all[q], (8, 128))
            turned = pltpu.roll(row, ((q + 8 - i) * GROUP) % 128, axis=1)
            cut = jnp.where(lane_place == q, turned, cut)
        for block in range(9):
            level = f * OWN - HALO + block * 8 + iota((8, 128), 0)
            root = jnp.sqrt(jnp.maximum(level, 0).astype(jnp.float32) / FA)
            ladder[pl.ds(block * 8, 8), :] = jnp.where(
                (level >= 1) & (level < cut), 2.0 * strength_first * root, 0.0
            )
        sub = iota((8, 128), 0).astype(jnp.float32)
        double = 2.0 * strength_second
        link = double * jnp.sqrt((2.0 * sub + 1.0) / FB)
        low_side = double * jnp.sqrt(2.0 * sub / FB)
        high_side = jnp.where(sub < 7.0, double * jnp.sqrt((2.0 * sub + 2.0) / FB), 0.0)

        wait_for(halo_recv.at[i], inb.at[i])

        for part, natural in ((0, nat_re), (1, nat_im)):
            for b in range(8):
                if b < 2:
                    piece = left[i, part, :, b * 128 : (b + 1) * 128]
                elif b < 6:
                    piece = inb[i, part, :, (b - 2) * 128 : (b - 1) * 128]
                else:
                    piece = right[i, part, :, (b - 6) * 128 : (b - 5) * 128]
                natural[b * 128 : (b + 1) * 128, :] = piece.T

        def first_term(n, c):
            for natural, vec, even in ((nat_re, vec_re, even_re), (nat_im, vec_im, even_im)):
                for j in range(4):
                    for t in range(2):
                        value = natural[pl.ds((n * 4 + j) * 16 + t, 8, stride=2), :]
                        place = pl.ds(pl.multiple_of((n * 4 + j) * 16 + t * 8, 8), 8)
                        vec[place, :] = value
                        even[place, :] = OMEGA[DEGREE] * value
            return c

        lax.fori_loop(0, LEVELS // 4, first_term, 0)
        for k in range(DEGREE - 1, -1, -1):
            series_step(k, i, (link, low_side, high_side))

        y = jnp.concatenate([y_re[...], y_im[...]], axis=1)
        y_hi = y.astype(jnp.bfloat16)
        y_lo = (y - y_hi.astype(jnp.float32)).astype(jnp.bfloat16)

        def product(a, b):
            return lax.dot_general(
                a, b, (((1,), (1,)), ((), ())), preferred_element_type=jnp.float32
            )

        mixed = (
            product(mix_hi[...], y_hi) + product(mix_hi[...], y_lo) + product(mix_lo[...], y_hi)
        )
        outb[i, 0] = mixed[:LANES]
        outb[i, 1] = mixed[LANES:]

        @pl.when(i < LAST)
        def _():
            for k in order:
                out_copy(i, k).start()

        @pl.when(i == LAST)
        def _():
            for h in range(HALVES):
                for k in order:
                    tail_copy(h, k).start()

        @pl.when(i < CHUNKS - AHEAD)
        def _():
            forward(i + AHEAD)

        return carry

    lax.fori_loop(0, CHUNKS, chunk, 0)

    def turn(bit):
        return rot[3 * bit], rot[3 * bit + 1], rot[3 * bit + 2]

    for place in range(9):
        coef_out[2 * CHUNKS + place] = rot[21 + place]
    for i in range(CHUNKS):
        real = jnp.ones((8, 128), jnp.float32)
        imag = jnp.zeros((8, 128), jnp.float32)
        for place in range(3):
            cosine, driven, kept = turn(4 + place)
            if (i >> place) & 1:
                real, imag = real * cosine, imag * cosine
            else:
                real, imag = imag * kept - real * driven, -real * kept - imag * driven
        coef_out[i] = real
        coef_out[CHUNKS + i] = imag

    def spot(q, i, half, col):
        return (
            q * CHUNKS + i,
            pl.ds(pl.multiple_of(half * 8, 8), 8),
            pl.ds(pl.multiple_of(col * 128, 128), 128),
        )

    def rotate_places(i, carry):
        wait_for(out_recv.at[i], inb.at[i])

        def unit(u, c):
            half, col = u // COL_TILES, u % COL_TILES
            spots = [spot(q, i, half, col) for q in range(PLACES)]
            real = [back[0, g, r, l] for g, r, l in spots]
            imag = [back[1, g, r, l] for g, r, l in spots]
            real, imag = butterfly(real, imag, [(place, turn(7 + place)) for place in range(3)])
            for q, (g, r, l) in enumerate(spots):
                back[0, g, r, l] = real[q]
                back[1, g, r, l] = imag[q]
            return c

        lax.fori_loop(0, 2 * COL_TILES, unit, 0)
        return carry

    lax.fori_loop(0, LAST, rotate_places, 0)

    def rotate_chunks(q, carry):
        def unit(u, c):
            half, col = u // COL_TILES, u % COL_TILES
            spots = [spot(q, i, half, col) for i in range(CHUNKS)]
            zero = jnp.zeros((8, 128), jnp.float32)
            real = [back[0, g, r, l] for g, r, l in spots[:LAST]] + [zero]
            imag = [back[1, g, r, l] for g, r, l in spots[:LAST]] + [zero]
            real, imag = butterfly(real, imag, [(place, turn(4 + place)) for place in range(3)])
            for i, (g, r, l) in enumerate(spots):
                back[0, g, r, l] = real[i]
                back[1, g, r, l] = imag[i]
            return c

        lax.fori_loop(0, 2 * COL_TILES, unit, 0)
        return carry

    lax.fori_loop(0, PLACES, rotate_chunks, 0)

    wait_for(cut_send, cut_all.at[pl.ds(0, PLACES - 1)])
    wait_for(in_send, inb.at[:, :, others, :])
    wait_for(halo_send, inb)
    wait_for(out_send, inb.at[pl.ds(0, LAST), :, others, :])

    for h in range(HALVES):
        wait_for(tail_recv.at[h], landed.at[:, pl.ds(0, LANES // HALVES), :])
        if h < HALVES - 1:

            def finish(col, carry):
                finish_tile(landed, back, back, coef_out, h, h, col)
                return carry

            lax.fori_loop(0, COL_TILES, finish, 0)
    wait_for(tail_send, landed.at[:, others, :])


def finish_tile(landed, partial, done, coef, half, target, col):
    cols = pl.ds(pl.multiple_of(col * 128, 128), 128)
    rows = [pl.ds(q * GROUP + half * 8, 8) for q in range(PLACES)]
    real = [landed[0, r, cols] for r in rows]
    imag = [landed[1, r, cols] for r in rows]
    base = 2 * CHUNKS
    turns = [(place, tuple(coef[base + 3 * place + e] for e in range(3))) for place in range(3)]
    real, imag = butterfly(real, imag, turns)
    source, place = pl.ds(half * 8, 8), pl.ds(target * 8, 8)
    for i in range(CHUNKS):
        k_real, k_imag = coef[i], coef[CHUNKS + i]
        for q in range(PLACES):
            g = q * CHUNKS + i
            new_real = partial[0, g, source, cols] + (k_real * real[q] - k_imag * imag[q])
            new_imag = partial[1, g, source, cols] + (k_real * imag[q] + k_imag * real[q])
            done[0, g, place, cols] = new_real
            done[1, g, place, cols] = new_imag


def last_kernel(back, landed, coef, out, done, ready_sem, done_sem):
    ready = (HALVES - 1) * 8
    parts = []
    for j in range(4):
        groups = pl.ds(j * 16, 16)
        parts.append(
            pltpu.make_async_copy(
                back.at[:, groups, pl.ds(0, ready), :],
                out.at[:, groups, pl.ds(0, ready), :],
                ready_sem,
            )
        )
    for part in parts:
        part.start()

    def store_copy(col):
        cols = pl.ds(pl.multiple_of(col * 128, 128), 128)
        return pltpu.make_async_copy(
            done.at[:, :, :, cols], out.at[:, :, pl.ds(ready, 8), cols], done_sem
        )

    def finish(col, carry):
        finish_tile(landed, back, done, coef, HALVES - 1, 0, col)
        store_copy(col).start()
        return carry

    lax.fori_loop(0, COL_TILES, finish, 0)
    first = back.at[:, :, pl.ds(0, ready), :]
    pltpu.make_async_copy(first, first, ready_sem).wait()
    pltpu.make_async_copy(done, done, done_sem).wait()


def per_device(
    amplitudes,
    cutoffs,
    coupling_first,
    coupling_second,
    frozen_coupling,
    frozen_bits,
    drive_bits,
    angles,
):
    f32 = jnp.float32
    padded = pltpu.VMEM((PADDED * FB, LANES), f32)
    dma = pltpu.SemaphoreType.DMA
    smem = pl.BlockSpec(memory_space=pltpu.SMEM)
    vmem = pl.BlockSpec(memory_space=pltpu.VMEM)
    back, landed, coef = pl.pallas_call(
        kernel,
        name="evolve_and_rotate",
        out_shape=[
            pltpu.VMEM((2, PLACES * CHUNKS, GROUP, COLS), f32),
            pltpu.VMEM((2, LANES, COLS), f32),
            pltpu.VMEM((2 * CHUNKS + 9, 8, 128), f32),
        ],
        in_specs=[
            pl.BlockSpec(memory_space=pl.ANY),
            pl.BlockSpec(memory_space=pltpu.VMEM),
            smem,
            smem,
            smem,
            smem,
            smem,
            smem,
        ],
        out_specs=[vmem, vmem, vmem],
        scratch_shapes=[
            pltpu.VMEM((CHUNKS, 2, LANES, COLS), f32),
            pltpu.VMEM((PLACES, 1, 128), jnp.int32),
            pltpu.VMEM((CHUNKS, 2, LANES, SIDE), f32),
            pltpu.VMEM((CHUNKS, 2, LANES, SIDE), f32),
            pltpu.VMEM((LEVELS * FB, LANES), f32),
            pltpu.VMEM((LEVELS * FB, LANES), f32),
            padded,
            padded,
            padded,
            padded,
            padded,
            padded,
            pltpu.VMEM((COLS, LANES), f32),
            pltpu.VMEM((COLS, LANES), f32),
            padded,
            pltpu.VMEM((72, LANES), f32),
            pltpu.VMEM((3 * SPINS, 8, 128), f32),
            pltpu.VMEM((2 * LANES, 2 * LANES), jnp.bfloat16),
            pltpu.VMEM((2 * LANES, 2 * LANES), jnp.bfloat16),
            pltpu.VMEM((CHUNKS, 2, LANES, COLS), f32),
            dma,
            dma((CHUNKS,)),
            dma,
            dma,
            dma,
            dma((CHUNKS,)),
            dma,
            dma((LAST,)),
            dma,
            dma((HALVES,)),
        ],
        compiler_params=pltpu.CompilerParams(
            collective_id=0, has_side_effects=True, vmem_limit_bytes=62_000_000
        ),
    )(
        amplitudes,
        cutoffs.reshape(PLACES, 1, 128),
        coupling_first,
        coupling_second,
        frozen_coupling,
        frozen_bits,
        drive_bits,
        angles,
    )
    rotated = pl.pallas_call(
        last_kernel,
        name="rotate_last",
        out_shape=jax.ShapeDtypeStruct((2, PLACES * CHUNKS, GROUP, COLS), f32),
        in_specs=[vmem, vmem, vmem],
        out_specs=pl.BlockSpec(memory_space=pl.ANY),
        scratch_shapes=[
            pltpu.VMEM((2, PLACES * CHUNKS, 8, COLS), f32),
            dma,
            dma,
        ],
        compiler_params=pltpu.CompilerParams(vmem_limit_bytes=16 << 20),
    )(back, landed, coef)
    return rotated.reshape(amplitudes.shape)


def solution(mesh):
    placed = (P(None, "spin", "fock"), P("spin"), P(), P(), P(), P(), P(), P())
    return jax.shard_map(
        per_device, mesh=mesh, in_specs=placed, out_specs=P(None, "spin", "fock"), check_vma=False
    )
```

```python
import math

import jax
import jax.numpy as jnp
from jax import lax
from jax.experimental import pallas as pl
from jax.experimental.pallas import tpu as pltpu
from jax.sharding import PartitionSpec as P

SPINS = 13
FA = 512
FB = 16
FROZEN = 16
DEGREE = 16
MESH_ID = pl.DeviceIdType.MESH

evolve_time = 12.0
diagonal_first = 0.06
diagonal_second = 0.04
ladder_first = 0.35
ladder_second = 0.1

PLACES = 8
CHUNKS = 8
GROUP = 16
LANES = PLACES * GROUP
OWN = 32
HALO = DEGREE
LEVELS = OWN + 2 * HALO
PADDED = LEVELS + 4
COLS = OWN * FB
SIDE = HALO * FB
LANE_BITS = (0, 1, 2, 3, 10, 11, 12)
AHEAD = 2
COL_TILES = COLS // 128
HALVES = GROUP // 8
LAST = CHUNKS - 1


def bessel_first(term_order, argument):
    running = 0.0
    addend = (argument / 2.0) ** term_order / math.factorial(term_order)
    for serial in range(80):
        running = running + addend
        addend = addend * -(argument * argument / 4.0) / ((serial + 1) * (serial + 1 + term_order))
    return running


OMEGA = [(1.0 if k == 0 else 2.0) * bessel_first(k, evolve_time) for k in range(DEGREE + 1)]


def iota(shape, dim):
    return lax.broadcasted_iota(jnp.int32, shape, dim)


def fill_rotations(angles, drive_bits, rot):
    for j in range(SPINS):
        angle = jnp.full((8, 128), angles[j], jnp.float32)
        phase = jnp.full((8, 128), drive_bits[j], jnp.int32).astype(jnp.float32)
        sine = jnp.sin(angle)
        rot[3 * j] = jnp.cos(angle)
        rot[3 * j + 1] = sine * phase
        rot[3 * j + 2] = sine * (1.0 - phase)


def fill_mixer(rot, mix_hi, mix_lo):
    def rows(step, carry):
        base = pl.multiple_of(step * 16, 16)
        out_lane = base + iota((16, 128), 0)
        in_lane = iota((16, 128), 1)
        real = jnp.ones((16, 128), jnp.float32)
        imag = jnp.zeros((16, 128), jnp.float32)
        for place, bit in enumerate(LANE_BITS):
            out_bit = (out_lane >> place) & 1
            in_bit = (in_lane >> place) & 1
            same = out_bit == in_bit
            cosine = jnp.concatenate([rot[3 * bit]] * 2, axis=0)
            driven = jnp.concatenate([rot[3 * bit + 1]] * 2, axis=0)
            kept = jnp.concatenate([rot[3 * bit + 2]] * 2, axis=0)
            f_real = jnp.where(same, cosine, jnp.where(out_bit == 1, driven, -driven))
            f_imag = jnp.where(same, 0.0, -kept)
            real, imag = real * f_real - imag * f_imag, real * f_imag + imag * f_real
        top = jnp.concatenate([real, -imag], axis=1)
        low = jnp.concatenate([imag, real], axis=1)
        for start, value in ((0, top), (128, low)):
            high = value.astype(jnp.bfloat16)
            rest = (value - high.astype(jnp.float32)).astype(jnp.bfloat16)
            mix_hi[pl.ds(start + base, 16), :] = high
            mix_lo[pl.ds(start + base, 16), :] = rest
        return carry

    lax.fori_loop(0, 8, rows, 0)


def fill_diagonal(fock_place, diag):
    def rows(n, carry):
        row = iota((16, 128), 0)
        m = 2 * (row % 8) + row // 8
        level = fock_place * OWN - HALO + n
        level_float = jnp.full((16, 128), level, jnp.int32).astype(jnp.float32)
        value = diagonal_first * (2.0 * level_float / (FA - 1) - 1.0) + diagonal_second * (
            2.0 * m.astype(jnp.float32) / (FB - 1) - 1.0
        )
        diag[pl.ds(pl.multiple_of(n * 16, 16), 16), :] = 2.0 * value
        return carry

    lax.fori_loop(0, PADDED, rows, 0)


def strengths(chunk, spin_place, coupling_first, coupling_second, frozen_coupling, frozen_bits):
    shape = (8, 128)
    lane = iota(shape, 1)
    config = (lane >> 4) * 1024 + (spin_place * CHUNKS + chunk) * GROUP + (lane & 15)
    first = jnp.zeros(shape, jnp.float32)
    second = jnp.zeros(shape, jnp.float32)
    total_first = jnp.zeros(shape, jnp.float32)
    total_second = jnp.zeros(shape, jnp.float32)
    for j in range(SPINS):
        sign = (1 - 2 * ((config >> j) & 1)).astype(jnp.float32)
        first = first + coupling_first[j] * sign
        second = second + coupling_second[j] * sign
        total_first = total_first + coupling_first[j]
        total_second = total_second + coupling_second[j]
    for k in range(FROZEN):
        sign = jnp.full(shape, 1 - 2 * frozen_bits[k], jnp.int32).astype(jnp.float32)
        first = first + frozen_coupling[k] * sign
        total_first = total_first + frozen_coupling[k]
    return ladder_first * first / total_first, ladder_second * second / total_second


def butterfly(real, imag, bits):
    count = len(real)
    for place, (cosine, driven, kept) in bits:
        step = 1 << place
        for low in range(count):
            if low & step:
                continue
            up = low | step
            lr, li, ur, ui = real[low], imag[low], real[up], imag[up]
            real[low] = cosine * lr - driven * ur + kept * ui
            imag[low] = cosine * li - driven * ui - kept * ur
            real[up] = cosine * ur + driven * lr + kept * li
            imag[up] = cosine * ui + driven * li - kept * lr
    return real, imag


def kernel(
    x,
    cutoffs,
    small_0,
    small_1,
    small_2,
    small_3,
    small_4,
    small_5,
    back,
    landed,
    coef_out,
    inb,
    cut_all,
    left,
    right,
    nat_re,
    nat_im,
    vec_re,
    vec_im,
    even_re,
    even_im,
    odd_re,
    odd_im,
    y_re,
    y_im,
    diag,
    ladder,
    rot,
    mix_hi,
    mix_lo,
    outb,
    in_send,
    in_recv,
    cut_send,
    cut_recv,
    halo_send,
    halo_recv,
    out_send,
    out_recv,
    tail_send,
    tail_recv,
    coupling_first,
    coupling_second,
    frozen_coupling,
    frozen_bits,
    drive_bits,
    angles,
    small_sem,
):
    s = lax.axis_index("spin")
    f = lax.axis_index("fock")
    f_left = (f + 15) % 16
    f_right = (f + 1) % 16

    barrier = pltpu.get_barrier_semaphore()
    for k in range(1, PLACES):
        pl.semaphore_signal(barrier, inc=1, device_id=((s + k) % PLACES, f), device_id_type=MESH_ID)
    for near in (f_left, f_right):
        pl.semaphore_signal(barrier, inc=1, device_id=(s, near), device_id_type=MESH_ID)
    pl.semaphore_wait(barrier, PLACES + 1)

    def cut_copy(k):
        p = (s + k) % PLACES
        if k == 0:
            return pltpu.make_async_copy(cutoffs.at[s], cut_all.at[s], cut_recv)
        return pltpu.make_async_remote_copy(
            src_ref=cutoffs.at[p],
            dst_ref=cut_all.at[s],
            send_sem=cut_send,
            recv_sem=cut_recv,
            device_id=(p, f),
            device_id_type=MESH_ID,
        )

    def in_copy(i, k):
        p = (s + k) % PLACES
        src = x.at[:, pl.ds(pl.multiple_of((p * CHUNKS + i) * GROUP, GROUP), GROUP), :]
        dst = inb.at[i, :, pl.ds(pl.multiple_of(s * GROUP, GROUP), GROUP), :]
        if k == 0:
            return pltpu.make_async_copy(src, dst, in_recv.at[i])
        return pltpu.make_async_remote_copy(
            src_ref=src,
            dst_ref=dst,
            send_sem=in_send,
            recv_sem=in_recv.at[i],
            device_id=(p, f),
            device_id_type=MESH_ID,
        )

    def halo_copy(i, side):
        if side == 0:
            src, dst, near = inb.at[i, :, :, pl.ds(COLS - SIDE, SIDE)], left.at[i], f_right
        else:
            src, dst, near = inb.at[i, :, :, pl.ds(0, SIDE)], right.at[i], f_left
        return pltpu.make_async_remote_copy(
            src_ref=src,
            dst_ref=dst,
            send_sem=halo_send,
            recv_sem=halo_recv.at[i],
            device_id=(s, near),
            device_id_type=MESH_ID,
        )

    def out_copy(i, k):
        p = (s + k) % PLACES
        src = outb.at[i, :, pl.ds(pl.multiple_of(p * GROUP, GROUP), GROUP), :]
        dst = back.at[:, s * CHUNKS + i]
        if k == 0:
            return pltpu.make_async_copy(src, dst, out_recv.at[i])
        return pltpu.make_async_remote_copy(
            src_ref=src,
            dst_ref=dst,
            send_sem=out_send,
            recv_sem=out_recv.at[i],
            device_id=(p, f),
            device_id_type=MESH_ID,
        )

    def tail_copy(h, k):
        p = (s + k) % PLACES
        src = outb.at[LAST, :, pl.ds(pl.multiple_of(p * GROUP + h * 8, 8), 8), :]
        dst = landed.at[:, pl.ds(pl.multiple_of(s * GROUP + h * 8, 8), 8), :]
        if k == 0:
            return pltpu.make_async_copy(src, dst, tail_recv.at[h])
        return pltpu.make_async_remote_copy(
            src_ref=src,
            dst_ref=dst,
            send_sem=tail_send,
            recv_sem=tail_recv.at[h],
            device_id=(p, f),
            device_id_type=MESH_ID,
        )

    def wait_for(sem, like):
        pltpu.make_async_copy(like, like, sem).wait()

    others = pl.ds(0, LANES - GROUP)

    order = (4, 3, 5, 2, 6, 1, 7, 0)
    for k in order:
        cut_copy(k).start()

    def start_in(i, carry):
        for k in order:
            in_copy(i, k).start()
        return carry

    lax.fori_loop(0, CHUNKS, start_in, 0)

    fetches = [
        pltpu.make_async_copy(src, dst, small_sem.at[j])
        for j, (src, dst) in enumerate(
            (
                (small_5, angles),
                (small_4, drive_bits),
                (small_0, coupling_first),
                (small_1, coupling_second),
                (small_2, frozen_coupling),
                (small_3, frozen_bits),
            )
        )
    ]
    for fetch in fetches:
        fetch.start()
    for fetch in fetches:
        fetch.wait()
    fill_rotations(angles, drive_bits, rot)
    fill_mixer(rot, mix_hi, mix_lo)
    fill_diagonal(f, diag)
    wait_for(cut_recv, cut_all)

    def forward(i):
        wait_for(in_recv.at[i], inb.at[i])
        halo_copy(i, 0).start()
        halo_copy(i, 1).start()

    for i in range(AHEAD):
        forward(i)

    def series_step(k, i, coef):
        link, low_side, high_side = coef
        source_re, source_im = (odd_re, odd_im) if k % 2 == 0 else (even_re, even_im)
        target_re, target_im = (even_re, even_im) if k % 2 == 0 else (odd_re, odd_im)
        start = HALO - k
        groups = -(-(OWN + 2 * k) // 4)

        def group(g, carry):
            n0 = start + 4 * g

            def tile(ref, j, t):
                return ref[pl.ds(pl.multiple_of((n0 + j) * 16 + t * 8, 8), 8), :]

            steps = [ladder[pl.ds(n0 + j, 8, stride=0), :] for j in range(5)]
            diagonal = [[tile(diag, j, t) for t in range(2)] for j in range(4)]
            for source, target, vec, sign, y in (
                (source_im, target_re, vec_re, 1, y_re),
                (source_re, target_im, vec_im, -1, y_im),
            ):
                p = [[tile(source, j, t) for t in range(2)] for j in range(-1, 5)]
                for j in range(4):
                    for t in range(2):
                        own = p[j + 1][t]
                        other = p[j + 1][1 - t]
                        far = pltpu.roll(other, 1 if t == 0 else 7, axis=0)
                        applied = (
                            diagonal[j][t] * own
                            + link * other
                            + (low_side if t == 0 else high_side) * far
                            + (steps[j] * p[j][t] + steps[j + 1] * p[j + 2][t])
                        )
                        if k == 0:
                            applied = 0.5 * applied
                        kept = OMEGA[k] * tile(vec, j, t)
                        if k < DEGREE - 1:
                            kept = kept + tile(target, j, t)
                        value = kept + applied if sign > 0 else kept - applied
                        if k == 0:
                            row = (n0 + j - HALO) * 16 + t
                            y[pl.ds(row, 8, stride=2), :] = value
                        else:
                            target[pl.ds(pl.multiple_of((n0 + j) * 16 + t * 8, 8), 8), :] = value
            return carry

        lax.fori_loop(0, groups, group, 0)

    def chunk(i, carry):
        strength_first, strength_second = strengths(
            i, s, coupling_first, coupling_second, frozen_coupling, frozen_bits
        )
        cut = jnp.zeros((8, 128), jnp.int32)
        lane_place = iota((8, 128), 1) >> 4
        for q in range(PLACES):
            row = jnp.broadcast_to(cut_all[q], (8, 128))
            turned = pltpu.roll(row, ((q + 8 - i) * GROUP) % 128, axis=1)
            cut = jnp.where(lane_place == q, turned, cut)
        for block in range(9):
            level = f * OWN - HALO + block * 8 + iota((8, 128), 0)
            root = jnp.sqrt(jnp.maximum(level, 0).astype(jnp.float32) / FA)
            ladder[pl.ds(block * 8, 8), :] = jnp.where(
                (level >= 1) & (level < cut), 2.0 * strength_first * root, 0.0
            )
        sub = iota((8, 128), 0).astype(jnp.float32)
        double = 2.0 * strength_second
        link = double * jnp.sqrt((2.0 * sub + 1.0) / FB)
        low_side = double * jnp.sqrt(2.0 * sub / FB)
        high_side = jnp.where(sub < 7.0, double * jnp.sqrt((2.0 * sub + 2.0) / FB), 0.0)

        wait_for(halo_recv.at[i], inb.at[i])

        for part, natural in ((0, nat_re), (1, nat_im)):
            for b in range(8):
                if b < 2:
                    piece = left[i, part, :, b * 128 : (b + 1) * 128]
                elif b < 6:
                    piece = inb[i, part, :, (b - 2) * 128 : (b - 1) * 128]
                else:
                    piece = right[i, part, :, (b - 6) * 128 : (b - 5) * 128]
                natural[b * 128 : (b + 1) * 128, :] = piece.T

        def first_term(n, c):
            for natural, vec, even in ((nat_re, vec_re, even_re), (nat_im, vec_im, even_im)):
                for j in range(4):
                    for t in range(2):
                        value = natural[pl.ds((n * 4 + j) * 16 + t, 8, stride=2), :]
                        place = pl.ds(pl.multiple_of((n * 4 + j) * 16 + t * 8, 8), 8)
                        vec[place, :] = value
                        even[place, :] = OMEGA[DEGREE] * value
            return c

        lax.fori_loop(0, LEVELS // 4, first_term, 0)
        for k in range(DEGREE - 1, -1, -1):
            series_step(k, i, (link, low_side, high_side))

        y = jnp.concatenate([y_re[...], y_im[...]], axis=1)
        y_hi = y.astype(jnp.bfloat16)
        y_lo = (y - y_hi.astype(jnp.float32)).astype(jnp.bfloat16)

        def product(a, b):
            return lax.dot_general(
                a, b, (((1,), (1,)), ((), ())), preferred_element_type=jnp.float32
            )

        mixed = (
            product(mix_hi[...], y_hi) + product(mix_hi[...], y_lo) + product(mix_lo[...], y_hi)
        )
        outb[i, 0] = mixed[:LANES]
        outb[i, 1] = mixed[LANES:]

        @pl.when(i < LAST)
        def _():
            for k in order:
                out_copy(i, k).start()

        @pl.when(i == LAST)
        def _():
            for h in range(HALVES):
                for k in order:
                    tail_copy(h, k).start()

        @pl.when(i < CHUNKS - AHEAD)
        def _():
            forward(i + AHEAD)

        return carry

    lax.fori_loop(0, CHUNKS, chunk, 0)

    def turn(bit):
        return rot[3 * bit], rot[3 * bit + 1], rot[3 * bit + 2]

    for place in range(9):
        coef_out[2 * CHUNKS + place] = rot[21 + place]
    for i in range(CHUNKS):
        real = jnp.ones((8, 128), jnp.float32)
        imag = jnp.zeros((8, 128), jnp.float32)
        for place in range(3):
            cosine, driven, kept = turn(4 + place)
            if (i >> place) & 1:
                real, imag = real * cosine, imag * cosine
            else:
                real, imag = imag * kept - real * driven, -real * kept - imag * driven
        coef_out[i] = real
        coef_out[CHUNKS + i] = imag

    def spot(q, i, half, col):
        return (
            q * CHUNKS + i,
            pl.ds(pl.multiple_of(half * 8, 8), 8),
            pl.ds(pl.multiple_of(col * 128, 128), 128),
        )

    def rotate_places(i, carry):
        wait_for(out_recv.at[i], inb.at[i])

        def unit(u, c):
            half, col = u // COL_TILES, u % COL_TILES
            spots = [spot(q, i, half, col) for q in range(PLACES)]
            real = [back[0, g, r, l] for g, r, l in spots]
            imag = [back[1, g, r, l] for g, r, l in spots]
            real, imag = butterfly(real, imag, [(place, turn(7 + place)) for place in range(3)])
            for q, (g, r, l) in enumerate(spots):
                back[0, g, r, l] = real[q]
                back[1, g, r, l] = imag[q]
            return c

        lax.fori_loop(0, 2 * COL_TILES, unit, 0)
        return carry

    lax.fori_loop(0, LAST, rotate_places, 0)

    def rotate_chunks(q, carry):
        def unit(u, c):
            half, col = u // COL_TILES, u % COL_TILES
            spots = [spot(q, i, half, col) for i in range(CHUNKS)]
            zero = jnp.zeros((8, 128), jnp.float32)
            real = [back[0, g, r, l] for g, r, l in spots[:LAST]] + [zero]
            imag = [back[1, g, r, l] for g, r, l in spots[:LAST]] + [zero]
            real, imag = butterfly(real, imag, [(place, turn(4 + place)) for place in range(3)])
            for i, (g, r, l) in enumerate(spots):
                back[0, g, r, l] = real[i]
                back[1, g, r, l] = imag[i]
            return c

        lax.fori_loop(0, 2 * COL_TILES, unit, 0)
        return carry

    lax.fori_loop(0, PLACES, rotate_chunks, 0)

    wait_for(cut_send, cut_all.at[pl.ds(0, PLACES - 1)])
    wait_for(in_send, inb.at[:, :, others, :])
    wait_for(halo_send, inb)
    wait_for(out_send, inb.at[pl.ds(0, LAST), :, others, :])

    for h in range(HALVES):
        wait_for(tail_recv.at[h], landed.at[:, pl.ds(0, LANES // HALVES), :])
        if h < HALVES - 1:

            def finish(col, carry):
                finish_tile(landed, back, back, coef_out, h, h, col)
                return carry

            lax.fori_loop(0, COL_TILES, finish, 0)
    wait_for(tail_send, landed.at[:, others, :])


def finish_tile(landed, partial, done, coef, half, target, col):
    cols = pl.ds(pl.multiple_of(col * 128, 128), 128)
    rows = [pl.ds(q * GROUP + half * 8, 8) for q in range(PLACES)]
    real = [landed[0, r, cols] for r in rows]
    imag = [landed[1, r, cols] for r in rows]
    base = 2 * CHUNKS
    turns = [(place, tuple(coef[base + 3 * place + e] for e in range(3))) for place in range(3)]
    real, imag = butterfly(real, imag, turns)
    source, place = pl.ds(half * 8, 8), pl.ds(target * 8, 8)
    for i in range(CHUNKS):
        k_real, k_imag = coef[i], coef[CHUNKS + i]
        for q in range(PLACES):
            g = q * CHUNKS + i
            new_real = partial[0, g, source, cols] + (k_real * real[q] - k_imag * imag[q])
            new_imag = partial[1, g, source, cols] + (k_real * imag[q] + k_imag * real[q])
            done[0, g, place, cols] = new_real
            done[1, g, place, cols] = new_imag


def last_kernel(back, landed, coef, out, done, ready_sem, done_sem):
    ready = (HALVES - 1) * 8
    parts = []
    for j in range(4):
        groups = pl.ds(j * 16, 16)
        parts.append(
            pltpu.make_async_copy(
                back.at[:, groups, pl.ds(0, ready), :],
                out.at[:, groups, pl.ds(0, ready), :],
                ready_sem,
            )
        )
    for part in parts:
        part.start()

    def store_copy(col):
        cols = pl.ds(pl.multiple_of(col * 128, 128), 128)
        return pltpu.make_async_copy(
            done.at[:, :, :, cols], out.at[:, :, pl.ds(ready, 8), cols], done_sem
        )

    def finish(col, carry):
        finish_tile(landed, back, done, coef, HALVES - 1, 0, col)
        store_copy(col).start()
        return carry

    lax.fori_loop(0, COL_TILES, finish, 0)
    first = back.at[:, :, pl.ds(0, ready), :]
    pltpu.make_async_copy(first, first, ready_sem).wait()
    pltpu.make_async_copy(done, done, done_sem).wait()


def per_device(
    amplitudes,
    cutoffs,
    coupling_first,
    coupling_second,
    frozen_coupling,
    frozen_bits,
    drive_bits,
    angles,
):
    f32 = jnp.float32
    padded = pltpu.VMEM((PADDED * FB, LANES), f32)
    dma = pltpu.SemaphoreType.DMA
    vmem = pl.BlockSpec(memory_space=pltpu.VMEM)
    back, landed, coef = pl.pallas_call(
        kernel,
        name="evolve_and_rotate",
        out_shape=[
            pltpu.VMEM((2, PLACES * CHUNKS, GROUP, COLS), f32),
            pltpu.VMEM((2, LANES, COLS), f32),
            pltpu.VMEM((2 * CHUNKS + 9, 8, 128), f32),
        ],
        in_specs=[
            pl.BlockSpec(memory_space=pl.ANY),
        ]
        * 8,
        out_specs=[vmem, vmem, vmem],
        scratch_shapes=[
            pltpu.VMEM((CHUNKS, 2, LANES, COLS), f32),
            pltpu.VMEM((PLACES, 1, 128), jnp.int32),
            pltpu.VMEM((CHUNKS, 2, LANES, SIDE), f32),
            pltpu.VMEM((CHUNKS, 2, LANES, SIDE), f32),
            pltpu.VMEM((LEVELS * FB, LANES), f32),
            pltpu.VMEM((LEVELS * FB, LANES), f32),
            padded,
            padded,
            padded,
            padded,
            padded,
            padded,
            pltpu.VMEM((COLS, LANES), f32),
            pltpu.VMEM((COLS, LANES), f32),
            padded,
            pltpu.VMEM((72, LANES), f32),
            pltpu.VMEM((3 * SPINS, 8, 128), f32),
            pltpu.VMEM((2 * LANES, 2 * LANES), jnp.bfloat16),
            pltpu.VMEM((2 * LANES, 2 * LANES), jnp.bfloat16),
            pltpu.VMEM((CHUNKS, 2, LANES, COLS), f32),
            dma,
            dma((CHUNKS,)),
            dma,
            dma,
            dma,
            dma((CHUNKS,)),
            dma,
            dma((LAST,)),
            dma,
            dma((HALVES,)),
            pltpu.SMEM((SPINS,), f32),
            pltpu.SMEM((SPINS,), f32),
            pltpu.SMEM((FROZEN,), f32),
            pltpu.SMEM((FROZEN,), jnp.int32),
            pltpu.SMEM((SPINS,), jnp.int32),
            pltpu.SMEM((SPINS,), f32),
            dma((6,)),
        ],
        compiler_params=pltpu.CompilerParams(
            collective_id=0, has_side_effects=True, vmem_limit_bytes=62_100_000
        ),
    )(
        amplitudes,
        cutoffs.reshape(PLACES, 1, 128),
        coupling_first,
        coupling_second,
        frozen_coupling,
        frozen_bits,
        drive_bits,
        angles,
    )
    rotated = pl.pallas_call(
        last_kernel,
        name="rotate_last",
        out_shape=jax.ShapeDtypeStruct((2, PLACES * CHUNKS, GROUP, COLS), f32),
        in_specs=[vmem, vmem, vmem],
        out_specs=pl.BlockSpec(memory_space=pl.ANY),
        scratch_shapes=[
            pltpu.VMEM((2, PLACES * CHUNKS, 8, COLS), f32),
            dma,
            dma,
        ],
        compiler_params=pltpu.CompilerParams(vmem_limit_bytes=16 << 20),
    )(back, landed, coef)
    return rotated.reshape(amplitudes.shape)


def solution(mesh):
    placed = (P(None, "spin", "fock"), P("spin"), P(), P(), P(), P(), P(), P())
    return jax.shard_map(
        per_device, mesh=mesh, in_specs=placed, out_specs=P(None, "spin", "fock"), check_vma=False
    )
```

```python
import math

import jax
import jax.numpy as jnp
from jax import lax
from jax.experimental import pallas as pl
from jax.experimental.pallas import tpu as pltpu
from jax.sharding import PartitionSpec as P

SPINS = 13
FA = 512
FB = 16
FROZEN = 16
DEGREE = 16
MESH_ID = pl.DeviceIdType.MESH

evolve_time = 12.0
diagonal_first = 0.06
diagonal_second = 0.04
ladder_first = 0.35
ladder_second = 0.1

PLACES = 8
CHUNKS = 8
GROUP = 16
LANES = PLACES * GROUP
OWN = 32
HALO = DEGREE
LEVELS = OWN + 2 * HALO
PADDED = LEVELS + 4
COLS = OWN * FB
SIDE = HALO * FB
LANE_BITS = (0, 1, 2, 3, 10, 11, 12)
AHEAD = 2
SPARE = 8
COL_TILES = COLS // 128
HALVES = GROUP // 8
LAST = CHUNKS - 1


def bessel_first(term_order, argument):
    running = 0.0
    addend = (argument / 2.0) ** term_order / math.factorial(term_order)
    for serial in range(80):
        running = running + addend
        addend = addend * -(argument * argument / 4.0) / ((serial + 1) * (serial + 1 + term_order))
    return running


OMEGA = [(1.0 if k == 0 else 2.0) * bessel_first(k, evolve_time) for k in range(DEGREE + 1)]


def iota(shape, dim):
    return lax.broadcasted_iota(jnp.int32, shape, dim)


def fill_rotations(angles, drive_bits, rot):
    for j in range(SPINS):
        angle = jnp.full((8, 128), angles[j], jnp.float32)
        phase = jnp.full((8, 128), drive_bits[j], jnp.int32).astype(jnp.float32)
        sine = jnp.sin(angle)
        rot[3 * j] = jnp.cos(angle)
        rot[3 * j + 1] = sine * phase
        rot[3 * j + 2] = sine * (1.0 - phase)


def fill_mixer(rot, mix_hi, mix_lo):
    def rows(step, carry):
        base = pl.multiple_of(step * 16, 16)
        out_lane = base + iota((16, 128), 0)
        in_lane = iota((16, 128), 1)
        real = jnp.ones((16, 128), jnp.float32)
        imag = jnp.zeros((16, 128), jnp.float32)
        for place, bit in enumerate(LANE_BITS):
            out_bit = (out_lane >> place) & 1
            in_bit = (in_lane >> place) & 1
            same = out_bit == in_bit
            cosine = jnp.concatenate([rot[3 * bit]] * 2, axis=0)
            driven = jnp.concatenate([rot[3 * bit + 1]] * 2, axis=0)
            kept = jnp.concatenate([rot[3 * bit + 2]] * 2, axis=0)
            f_real = jnp.where(same, cosine, jnp.where(out_bit == 1, driven, -driven))
            f_imag = jnp.where(same, 0.0, -kept)
            real, imag = real * f_real - imag * f_imag, real * f_imag + imag * f_real
        top = jnp.concatenate([real, -imag], axis=1)
        low = jnp.concatenate([imag, real], axis=1)
        for start, value in ((0, top), (128, low)):
            high = value.astype(jnp.bfloat16)
            rest = (value - high.astype(jnp.float32)).astype(jnp.bfloat16)
            mix_hi[pl.ds(start + base, 16), :] = high
            mix_lo[pl.ds(start + base, 16), :] = rest
        return carry

    lax.fori_loop(0, 8, rows, 0)


def fill_diagonal(fock_place, diag):
    def rows(n, carry):
        row = iota((16, 128), 0)
        m = 2 * (row % 8) + row // 8
        level = fock_place * OWN - HALO + n
        level_float = jnp.full((16, 128), level, jnp.int32).astype(jnp.float32)
        value = diagonal_first * (2.0 * level_float / (FA - 1) - 1.0) + diagonal_second * (
            2.0 * m.astype(jnp.float32) / (FB - 1) - 1.0
        )
        diag[pl.ds(pl.multiple_of(n * 16, 16), 16), :] = 2.0 * value
        return carry

    lax.fori_loop(0, PADDED, rows, 0)


def strengths(chunk, spin_place, coupling_first, coupling_second, frozen_coupling, frozen_bits):
    shape = (8, 128)
    lane = iota(shape, 1)
    config = (lane >> 4) * 1024 + (spin_place * CHUNKS + chunk) * GROUP + (lane & 15)
    first = jnp.zeros(shape, jnp.float32)
    second = jnp.zeros(shape, jnp.float32)
    total_first = jnp.zeros(shape, jnp.float32)
    total_second = jnp.zeros(shape, jnp.float32)
    for j in range(SPINS):
        sign = (1 - 2 * ((config >> j) & 1)).astype(jnp.float32)
        first = first + coupling_first[j] * sign
        second = second + coupling_second[j] * sign
        total_first = total_first + coupling_first[j]
        total_second = total_second + coupling_second[j]
    for k in range(FROZEN):
        sign = jnp.full(shape, 1 - 2 * frozen_bits[k], jnp.int32).astype(jnp.float32)
        first = first + frozen_coupling[k] * sign
        total_first = total_first + frozen_coupling[k]
    return ladder_first * first / total_first, ladder_second * second / total_second


def butterfly(real, imag, bits):
    count = len(real)
    for place, (cosine, driven, kept) in bits:
        step = 1 << place
        for low in range(count):
            if low & step:
                continue
            up = low | step
            lr, li, ur, ui = real[low], imag[low], real[up], imag[up]
            real[low] = cosine * lr - driven * ur + kept * ui
            imag[low] = cosine * li - driven * ui - kept * ur
            real[up] = cosine * ur + driven * lr + kept * li
            imag[up] = cosine * ui + driven * li - kept * lr
    return real, imag


def kernel(
    x,
    cutoffs,
    small_0,
    small_1,
    small_2,
    small_3,
    small_4,
    small_5,
    back,
    landed,
    coef_out,
    inb,
    cut_all,
    left,
    right,
    nat_re,
    nat_im,
    vec_re,
    vec_im,
    even_re,
    even_im,
    odd_re,
    odd_im,
    y_re,
    y_im,
    diag,
    ladder,
    rot,
    mix_hi,
    mix_lo,
    outb,
    in_send,
    in_recv,
    cut_send,
    cut_recv,
    halo_send,
    halo_recv,
    out_send,
    out_recv,
    tail_send,
    tail_recv,
    coupling_first,
    coupling_second,
    frozen_coupling,
    frozen_bits,
    drive_bits,
    angles,
    small_sem,
):
    s = lax.axis_index("spin")
    f = lax.axis_index("fock")
    f_left = (f + 15) % 16
    f_right = (f + 1) % 16

    barrier = pltpu.get_barrier_semaphore()
    for k in range(1, PLACES):
        pl.semaphore_signal(barrier, inc=1, device_id=((s + k) % PLACES, f), device_id_type=MESH_ID)
    for near in (f_left, f_right):
        pl.semaphore_signal(barrier, inc=1, device_id=(s, near), device_id_type=MESH_ID)
    pl.semaphore_wait(barrier, PLACES + 1)

    def cut_copy(k):
        p = (s + k) % PLACES
        if k == 0:
            return pltpu.make_async_copy(cutoffs.at[s], cut_all.at[s], cut_recv)
        return pltpu.make_async_remote_copy(
            src_ref=cutoffs.at[p],
            dst_ref=cut_all.at[s],
            send_sem=cut_send,
            recv_sem=cut_recv,
            device_id=(p, f),
            device_id_type=MESH_ID,
        )

    def in_copy(i, k):
        p = (s + k) % PLACES
        src = x.at[:, pl.ds(pl.multiple_of((p * CHUNKS + i) * GROUP, GROUP), GROUP), :]
        dst = inb.at[i, :, pl.ds(pl.multiple_of(s * GROUP, GROUP), GROUP), :]
        if k == 0:
            return pltpu.make_async_copy(src, dst, in_recv.at[i])
        return pltpu.make_async_remote_copy(
            src_ref=src,
            dst_ref=dst,
            send_sem=in_send,
            recv_sem=in_recv.at[i],
            device_id=(p, f),
            device_id_type=MESH_ID,
        )

    def halo_copy(i, side):
        if side == 0:
            src, dst, near = inb.at[i, :, :, pl.ds(COLS - SIDE, SIDE)], left.at[i], f_right
        else:
            src, dst, near = inb.at[i, :, :, pl.ds(0, SIDE)], right.at[i], f_left
        return pltpu.make_async_remote_copy(
            src_ref=src,
            dst_ref=dst,
            send_sem=halo_send,
            recv_sem=halo_recv.at[i],
            device_id=(s, near),
            device_id_type=MESH_ID,
        )

    def out_copy(i, k):
        p = (s + k) % PLACES
        src = outb.at[i, :, pl.ds(pl.multiple_of(p * GROUP, GROUP), GROUP), :]
        dst = back.at[:, s * CHUNKS + i]
        if k == 0:
            return pltpu.make_async_copy(src, dst, out_recv.at[i])
        return pltpu.make_async_remote_copy(
            src_ref=src,
            dst_ref=dst,
            send_sem=out_send,
            recv_sem=out_recv.at[i],
            device_id=(p, f),
            device_id_type=MESH_ID,
        )

    def tail_copy(h, k):
        p = (s + k) % PLACES
        src = outb.at[LAST, :, pl.ds(pl.multiple_of(p * GROUP + h * 8, 8), 8), :]
        dst = landed.at[:, pl.ds(pl.multiple_of(s * GROUP + h * 8, 8), 8), :]
        if k == 0:
            return pltpu.make_async_copy(src, dst, tail_recv.at[h])
        return pltpu.make_async_remote_copy(
            src_ref=src,
            dst_ref=dst,
            send_sem=tail_send,
            recv_sem=tail_recv.at[h],
            device_id=(p, f),
            device_id_type=MESH_ID,
        )

    def wait_for(sem, like):
        pltpu.make_async_copy(like, like, sem).wait()

    others = pl.ds(0, LANES - GROUP)

    order = (4, 3, 5, 2, 6, 1, 7, 0)
    for k in order:
        cut_copy(k).start()

    def start_in(i, carry):
        for k in order:
            in_copy(i, k).start()
        return carry

    lax.fori_loop(0, CHUNKS, start_in, 0)

    fetches = [
        pltpu.make_async_copy(src, dst, small_sem.at[j])
        for j, (src, dst) in enumerate(
            (
                (small_5, angles),
                (small_4, drive_bits),
                (small_0, coupling_first),
                (small_1, coupling_second),
                (small_2, frozen_coupling),
                (small_3, frozen_bits),
            )
        )
    ]
    for fetch in fetches:
        fetch.start()
    for fetch in fetches:
        fetch.wait()
    fill_rotations(angles, drive_bits, rot)
    fill_mixer(rot, mix_hi, mix_lo)
    fill_diagonal(f, diag)
    wait_for(cut_recv, cut_all)

    def forward(i):
        wait_for(in_recv.at[i], inb.at[i])
        halo_copy(i, 0).start()
        halo_copy(i, 1).start()

    for i in range(AHEAD):
        forward(i)

    def series_step(k, i, coef):
        link, low_side, high_side = coef
        source_re, source_im = (odd_re, odd_im) if k % 2 == 0 else (even_re, even_im)
        target_re, target_im = (even_re, even_im) if k % 2 == 0 else (odd_re, odd_im)
        start = HALO - k
        groups = -(-(OWN + 2 * k) // 4)

        def group(g, carry):
            n0 = start + 4 * g

            def tile(ref, j, t):
                return ref[pl.ds(pl.multiple_of((n0 + j) * 16 + t * 8, 8), 8), :]

            steps = [ladder[pl.ds(n0 + j, 8, stride=0), :] for j in range(5)]
            diagonal = [[tile(diag, j, t) for t in range(2)] for j in range(4)]
            for source, target, vec, sign, y in (
                (source_im, target_re, vec_re, 1, y_re),
                (source_re, target_im, vec_im, -1, y_im),
            ):
                p = [[tile(source, j, t) for t in range(2)] for j in range(-1, 5)]
                for j in range(4):
                    for t in range(2):
                        own = p[j + 1][t]
                        other = p[j + 1][1 - t]
                        far = pltpu.roll(other, 1 if t == 0 else 7, axis=0)
                        applied = (
                            diagonal[j][t] * own
                            + link * other
                            + (low_side if t == 0 else high_side) * far
                            + (steps[j] * p[j][t] + steps[j + 1] * p[j + 2][t])
                        )
                        if k == 0:
                            applied = 0.5 * applied
                        kept = OMEGA[k] * tile(vec, j, t)
                        if k < DEGREE - 1:
                            kept = kept + tile(target, j, t)
                        value = kept + applied if sign > 0 else kept - applied
                        if k == 0:
                            row = (n0 + j - HALO) * 16 + t
                            y[pl.ds(row, 8, stride=2), :] = value
                        else:
                            target[pl.ds(pl.multiple_of((n0 + j) * 16 + t * 8, 8), 8), :] = value
            return carry

        lax.fori_loop(0, groups, group, 0)

    def chunk(i, carry):
        strength_first, strength_second = strengths(
            i, s, coupling_first, coupling_second, frozen_coupling, frozen_bits
        )
        cut = jnp.zeros((8, 128), jnp.int32)
        lane_place = iota((8, 128), 1) >> 4
        for q in range(PLACES):
            row = jnp.broadcast_to(cut_all[q], (8, 128))
            turned = pltpu.roll(row, ((q + 8 - i) * GROUP) % 128, axis=1)
            cut = jnp.where(lane_place == q, turned, cut)
        for block in range(9):
            level = f * OWN - HALO + block * 8 + iota((8, 128), 0)
            root = jnp.sqrt(jnp.maximum(level, 0).astype(jnp.float32) / FA)
            ladder[pl.ds(block * 8, 8), :] = jnp.where(
                (level >= 1) & (level < cut), 2.0 * strength_first * root, 0.0
            )
        sub = iota((8, 128), 0).astype(jnp.float32)
        double = 2.0 * strength_second
        link = double * jnp.sqrt((2.0 * sub + 1.0) / FB)
        low_side = double * jnp.sqrt(2.0 * sub / FB)
        high_side = jnp.where(sub < 7.0, double * jnp.sqrt((2.0 * sub + 2.0) / FB), 0.0)

        wait_for(halo_recv.at[i], inb.at[i])

        for part, natural in ((0, nat_re), (1, nat_im)):
            for b in range(8):
                if b < 2:
                    piece = left[i, part, :, b * 128 : (b + 1) * 128]
                elif b < 6:
                    piece = inb[i, part, :, (b - 2) * 128 : (b - 1) * 128]
                else:
                    piece = right[i, part, :, (b - 6) * 128 : (b - 5) * 128]
                natural[b * 128 : (b + 1) * 128, :] = piece.T

        def first_term(n, c):
            for natural, vec, even in ((nat_re, vec_re, even_re), (nat_im, vec_im, even_im)):
                for j in range(4):
                    for t in range(2):
                        value = natural[pl.ds((n * 4 + j) * 16 + t, 8, stride=2), :]
                        place = pl.ds(pl.multiple_of((n * 4 + j) * 16 + t * 8, 8), 8)
                        vec[place, :] = value
                        even[place, :] = OMEGA[DEGREE] * value
            return c

        lax.fori_loop(0, LEVELS // 4, first_term, 0)
        for k in range(DEGREE - 1, -1, -1):
            series_step(k, i, (link, low_side, high_side))

        y = jnp.concatenate([y_re[:COLS, :], y_im[:COLS, :]], axis=1)
        y_hi = y.astype(jnp.bfloat16)
        y_lo = (y - y_hi.astype(jnp.float32)).astype(jnp.bfloat16)

        def product(a, b):
            return lax.dot_general(
                a, b, (((1,), (1,)), ((), ())), preferred_element_type=jnp.float32
            )

        mixed = (
            product(mix_hi[...], y_hi) + product(mix_hi[...], y_lo) + product(mix_lo[...], y_hi)
        )
        outb[i, 0] = mixed[:LANES]
        outb[i, 1] = mixed[LANES:]

        @pl.when(i < LAST)
        def _():
            for k in order:
                out_copy(i, k).start()

        @pl.when(i == LAST)
        def _():
            for h in range(HALVES):
                for k in order:
                    tail_copy(h, k).start()

        @pl.when(i < CHUNKS - AHEAD)
        def _():
            forward(i + AHEAD)

        return carry

    lax.fori_loop(0, CHUNKS, chunk, 0)

    def turn(bit):
        return rot[3 * bit], rot[3 * bit + 1], rot[3 * bit + 2]

    for place in range(9):
        coef_out[2 * CHUNKS + place] = rot[21 + place]
    for i in range(CHUNKS):
        real = jnp.ones((8, 128), jnp.float32)
        imag = jnp.zeros((8, 128), jnp.float32)
        for place in range(3):
            cosine, driven, kept = turn(4 + place)
            if (i >> place) & 1:
                real, imag = real * cosine, imag * cosine
            else:
                real, imag = imag * kept - real * driven, -real * kept - imag * driven
        coef_out[i] = real
        coef_out[CHUNKS + i] = imag

    def spot(q, i, half, col):
        return (
            q * CHUNKS + i,
            pl.ds(pl.multiple_of(half * 8, 8), 8),
            pl.ds(pl.multiple_of(col * 128, 128), 128),
        )

    def rotate_places(i, carry):
        wait_for(out_recv.at[i], inb.at[i])

        def unit(u, c):
            half, col = u // COL_TILES, u % COL_TILES
            spots = [spot(q, i, half, col) for q in range(PLACES)]
            real = [back[0, g, r, l] for g, r, l in spots]
            imag = [back[1, g, r, l] for g, r, l in spots]
            real, imag = butterfly(real, imag, [(place, turn(7 + place)) for place in range(3)])
            for q, (g, r, l) in enumerate(spots):
                back[0, g, r, l] = real[q]
                back[1, g, r, l] = imag[q]
            return c

        lax.fori_loop(0, 2 * COL_TILES, unit, 0)
        return carry

    lax.fori_loop(0, LAST, rotate_places, 0)

    def rotate_chunks(q, carry):
        def unit(u, c):
            half, col = u // COL_TILES, u % COL_TILES
            spots = [spot(q, i, half, col) for i in range(CHUNKS)]
            zero = jnp.zeros((8, 128), jnp.float32)
            real = [back[0, g, r, l] for g, r, l in spots[:LAST]] + [zero]
            imag = [back[1, g, r, l] for g, r, l in spots[:LAST]] + [zero]
            real, imag = butterfly(real, imag, [(place, turn(4 + place)) for place in range(3)])
            for i, (g, r, l) in enumerate(spots):
                back[0, g, r, l] = real[i]
                back[1, g, r, l] = imag[i]
            return c

        lax.fori_loop(0, 2 * COL_TILES, unit, 0)
        return carry

    lax.fori_loop(0, PLACES, rotate_chunks, 0)

    wait_for(cut_send, cut_all.at[pl.ds(0, PLACES - 1)])
    wait_for(in_send, inb.at[:, :, others, :])
    wait_for(halo_send, inb)
    wait_for(out_send, inb.at[pl.ds(0, LAST), :, others, :])

    for h in range(HALVES):
        wait_for(tail_recv.at[h], landed.at[:, pl.ds(0, LANES // HALVES), :])
        if h < HALVES - 1:

            def finish(col, carry):
                finish_tile(landed, back, back, coef_out, h, h, col)
                return carry

            lax.fori_loop(0, COL_TILES, finish, 0)
    wait_for(tail_send, landed.at[:, others, :])


def finish_tile(landed, partial, done, coef, half, target, col):
    cols = pl.ds(pl.multiple_of(col * 128, 128), 128)
    rows = [pl.ds(q * GROUP + half * 8, 8) for q in range(PLACES)]
    real = [landed[0, r, cols] for r in rows]
    imag = [landed[1, r, cols] for r in rows]
    base = 2 * CHUNKS
    turns = [(place, tuple(coef[base + 3 * place + e] for e in range(3))) for place in range(3)]
    real, imag = butterfly(real, imag, turns)
    source, place = pl.ds(half * 8, 8), pl.ds(target * 8, 8)
    for i in range(CHUNKS):
        k_real, k_imag = coef[i], coef[CHUNKS + i]
        for q in range(PLACES):
            g = q * CHUNKS + i
            new_real = partial[0, g, source, cols] + (k_real * real[q] - k_imag * imag[q])
            new_imag = partial[1, g, source, cols] + (k_real * imag[q] + k_imag * real[q])
            done[0, g, place, cols] = new_real
            done[1, g, place, cols] = new_imag


def last_kernel(back, landed, coef, out, done, ready_sem, done_sem):
    ready = (HALVES - 1) * 8
    parts = []
    for j in range(4):
        groups = pl.ds(j * 16, 16)
        parts.append(
            pltpu.make_async_copy(
                back.at[:, groups, pl.ds(0, ready), :],
                out.at[:, groups, pl.ds(0, ready), :],
                ready_sem,
            )
        )
    for part in parts:
        part.start()

    def store_copy(col):
        cols = pl.ds(pl.multiple_of(col * 128, 128), 128)
        return pltpu.make_async_copy(
            done.at[:, :, :, cols], out.at[:, :, pl.ds(ready, 8), cols], done_sem
        )

    def finish(col, carry):
        finish_tile(landed, back, done, coef, HALVES - 1, 0, col)
        store_copy(col).start()
        return carry

    lax.fori_loop(0, COL_TILES, finish, 0)
    first = back.at[:, :, pl.ds(0, ready), :]
    pltpu.make_async_copy(first, first, ready_sem).wait()
    pltpu.make_async_copy(done, done, done_sem).wait()


def per_device(
    amplitudes,
    cutoffs,
    coupling_first,
    coupling_second,
    frozen_coupling,
    frozen_bits,
    drive_bits,
    angles,
):
    f32 = jnp.float32
    padded = pltpu.VMEM((PADDED * FB, LANES), f32)
    dma = pltpu.SemaphoreType.DMA
    vmem = pl.BlockSpec(memory_space=pltpu.VMEM)
    back, landed, coef = pl.pallas_call(
        kernel,
        name="evolve_and_rotate",
        out_shape=[
            pltpu.VMEM((2, PLACES * CHUNKS, GROUP, COLS), f32),
            pltpu.VMEM((2, LANES, COLS), f32),
            pltpu.VMEM((2 * CHUNKS + 9, 8, 128), f32),
        ],
        in_specs=[
            pl.BlockSpec(memory_space=pl.ANY),
        ]
        * 8,
        out_specs=[vmem, vmem, vmem],
        scratch_shapes=[
            pltpu.VMEM((CHUNKS, 2, LANES, COLS), f32),
            pltpu.VMEM((PLACES, 1, 128), jnp.int32),
            pltpu.VMEM((CHUNKS, 2, LANES, SIDE), f32),
            pltpu.VMEM((CHUNKS, 2, LANES, SIDE), f32),
            pltpu.VMEM((LEVELS * FB + SPARE, LANES), f32),
            pltpu.VMEM((LEVELS * FB + SPARE, LANES), f32),
            padded,
            padded,
            padded,
            padded,
            padded,
            padded,
            pltpu.VMEM((COLS + SPARE, LANES), f32),
            pltpu.VMEM((COLS + SPARE, LANES), f32),
            padded,
            pltpu.VMEM((72 + SPARE, LANES), f32),
            pltpu.VMEM((3 * SPINS, 8, 128), f32),
            pltpu.VMEM((2 * LANES, 2 * LANES), jnp.bfloat16),
            pltpu.VMEM((2 * LANES, 2 * LANES), jnp.bfloat16),
            pltpu.VMEM((CHUNKS, 2, LANES, COLS), f32),
            dma,
            dma((CHUNKS,)),
            dma,
            dma,
            dma,
            dma((CHUNKS,)),
            dma,
            dma((LAST,)),
            dma,
            dma((HALVES,)),
            pltpu.SMEM((SPINS,), f32),
            pltpu.SMEM((SPINS,), f32),
            pltpu.SMEM((FROZEN,), f32),
            pltpu.SMEM((FROZEN,), jnp.int32),
            pltpu.SMEM((SPINS,), jnp.int32),
            pltpu.SMEM((SPINS,), f32),
            dma((6,)),
        ],
        compiler_params=pltpu.CompilerParams(
            collective_id=0, has_side_effects=True, vmem_limit_bytes=62_100_000
        ),
    )(
        amplitudes,
        cutoffs.reshape(PLACES, 1, 128),
        coupling_first,
        coupling_second,
        frozen_coupling,
        frozen_bits,
        drive_bits,
        angles,
    )
    rotated = pl.pallas_call(
        last_kernel,
        name="rotate_last",
        out_shape=jax.ShapeDtypeStruct((2, PLACES * CHUNKS, GROUP, COLS), f32),
        in_specs=[vmem, vmem, vmem],
        out_specs=pl.BlockSpec(memory_space=pl.ANY),
        scratch_shapes=[
            pltpu.VMEM((2, PLACES * CHUNKS, 8, COLS), f32),
            dma,
            dma,
        ],
        compiler_params=pltpu.CompilerParams(vmem_limit_bytes=16 << 20),
    )(back, landed, coef)
    return rotated.reshape(amplitudes.shape)


def solution(mesh):
    placed = (P(None, "spin", "fock"), P("spin"), P(), P(), P(), P(), P(), P())
    return jax.shard_map(
        per_device, mesh=mesh, in_specs=placed, out_specs=P(None, "spin", "fock"), check_vma=False
    )
```

```python
import math

import jax
import jax.numpy as jnp
from jax import lax
from jax.experimental import pallas as pl
from jax.experimental.pallas import tpu as pltpu
from jax.sharding import PartitionSpec as P

SPINS = 13
FA = 512
FB = 16
FROZEN = 16
DEGREE = 16
MESH_ID = pl.DeviceIdType.MESH

evolve_time = 12.0
diagonal_first = 0.06
diagonal_second = 0.04
ladder_first = 0.35
ladder_second = 0.1

PLACES = 8
CHUNKS = 8
GROUP = 16
LANES = PLACES * GROUP
OWN = 32
HALO = DEGREE
LEVELS = OWN + 2 * HALO
PADDED = LEVELS + 4
COLS = OWN * FB
SIDE = HALO * FB
LANE_BITS = (0, 1, 2, 3, 10, 11, 12)
AHEAD = 3
COL_TILES = COLS // 128
HALVES = GROUP // 8
LAST = CHUNKS - 1


def bessel_first(term_order, argument):
    running = 0.0
    addend = (argument / 2.0) ** term_order / math.factorial(term_order)
    for serial in range(80):
        running = running + addend
        addend = addend * -(argument * argument / 4.0) / ((serial + 1) * (serial + 1 + term_order))
    return running


OMEGA = [(1.0 if k == 0 else 2.0) * bessel_first(k, evolve_time) for k in range(DEGREE + 1)]


def iota(shape, dim):
    return lax.broadcasted_iota(jnp.int32, shape, dim)


def fill_rotations(angles, drive_bits, rot):
    for j in range(SPINS):
        angle = jnp.full((8, 128), angles[j], jnp.float32)
        phase = jnp.full((8, 128), drive_bits[j], jnp.int32).astype(jnp.float32)
        sine = jnp.sin(angle)
        rot[3 * j] = jnp.cos(angle)
        rot[3 * j + 1] = sine * phase
        rot[3 * j + 2] = sine * (1.0 - phase)


def fill_mixer(rot, mix_hi, mix_lo):
    def rows(step, carry):
        base = pl.multiple_of(step * 16, 16)
        out_lane = base + iota((16, 128), 0)
        in_lane = iota((16, 128), 1)
        real = jnp.ones((16, 128), jnp.float32)
        imag = jnp.zeros((16, 128), jnp.float32)
        for place, bit in enumerate(LANE_BITS):
            out_bit = (out_lane >> place) & 1
            in_bit = (in_lane >> place) & 1
            same = out_bit == in_bit
            cosine = jnp.concatenate([rot[3 * bit]] * 2, axis=0)
            driven = jnp.concatenate([rot[3 * bit + 1]] * 2, axis=0)
            kept = jnp.concatenate([rot[3 * bit + 2]] * 2, axis=0)
            f_real = jnp.where(same, cosine, jnp.where(out_bit == 1, driven, -driven))
            f_imag = jnp.where(same, 0.0, -kept)
            real, imag = real * f_real - imag * f_imag, real * f_imag + imag * f_real
        top = jnp.concatenate([real, -imag], axis=1)
        low = jnp.concatenate([imag, real], axis=1)
        for start, value in ((0, top), (128, low)):
            high = value.astype(jnp.bfloat16)
            rest = (value - high.astype(jnp.float32)).astype(jnp.bfloat16)
            mix_hi[pl.ds(start + base, 16), :] = high
            mix_lo[pl.ds(start + base, 16), :] = rest
        return carry

    lax.fori_loop(0, 8, rows, 0)


def fill_diagonal(fock_place, diag):
    def rows(n, carry):
        row = iota((16, 128), 0)
        m = 2 * (row % 8) + row // 8
        level = fock_place * OWN - HALO + n
        level_float = jnp.full((16, 128), level, jnp.int32).astype(jnp.float32)
        value = diagonal_first * (2.0 * level_float / (FA - 1) - 1.0) + diagonal_second * (
            2.0 * m.astype(jnp.float32) / (FB - 1) - 1.0
        )
        diag[pl.ds(pl.multiple_of(n * 16, 16), 16), :] = 2.0 * value
        return carry

    lax.fori_loop(0, PADDED, rows, 0)


def strengths(chunk, spin_place, coupling_first, coupling_second, frozen_coupling, frozen_bits):
    shape = (8, 128)
    lane = iota(shape, 1)
    config = (lane >> 4) * 1024 + (spin_place * CHUNKS + chunk) * GROUP + (lane & 15)
    first = jnp.zeros(shape, jnp.float32)
    second = jnp.zeros(shape, jnp.float32)
    total_first = jnp.zeros(shape, jnp.float32)
    total_second = jnp.zeros(shape, jnp.float32)
    for j in range(SPINS):
        sign = (1 - 2 * ((config >> j) & 1)).astype(jnp.float32)
        first = first + coupling_first[j] * sign
        second = second + coupling_second[j] * sign
        total_first = total_first + coupling_first[j]
        total_second = total_second + coupling_second[j]
    for k in range(FROZEN):
        sign = jnp.full(shape, 1 - 2 * frozen_bits[k], jnp.int32).astype(jnp.float32)
        first = first + frozen_coupling[k] * sign
        total_first = total_first + frozen_coupling[k]
    return ladder_first * first / total_first, ladder_second * second / total_second


def butterfly(real, imag, bits):
    count = len(real)
    for place, (cosine, driven, kept) in bits:
        step = 1 << place
        for low in range(count):
            if low & step:
                continue
            up = low | step
            lr, li, ur, ui = real[low], imag[low], real[up], imag[up]
            real[low] = cosine * lr - driven * ur + kept * ui
            imag[low] = cosine * li - driven * ui - kept * ur
            real[up] = cosine * ur + driven * lr + kept * li
            imag[up] = cosine * ui + driven * li - kept * lr
    return real, imag


def kernel(
    x,
    cutoffs,
    small_0,
    small_1,
    small_2,
    small_3,
    small_4,
    small_5,
    back,
    landed,
    coef_out,
    inb,
    cut_all,
    left,
    right,
    nat_re,
    nat_im,
    vec_re,
    vec_im,
    even_re,
    even_im,
    odd_re,
    odd_im,
    y_re,
    y_im,
    diag,
    ladder,
    rot,
    mix_hi,
    mix_lo,
    outb,
    in_send,
    in_recv,
    cut_send,
    cut_recv,
    halo_send,
    halo_recv,
    out_send,
    out_recv,
    tail_send,
    tail_recv,
    coupling_first,
    coupling_second,
    frozen_coupling,
    frozen_bits,
    drive_bits,
    angles,
    small_sem,
):
    s = lax.axis_index("spin")
    f = lax.axis_index("fock")
    f_left = (f + 15) % 16
    f_right = (f + 1) % 16

    barrier = pltpu.get_barrier_semaphore()
    for k in (4, 3, 5, 2, 6, 7, 1):
        pl.semaphore_signal(barrier, inc=1, device_id=((s + k) % PLACES, f), device_id_type=MESH_ID)
    for near in (f_left, f_right):
        pl.semaphore_signal(barrier, inc=1, device_id=(s, near), device_id_type=MESH_ID)
    pl.semaphore_wait(barrier, PLACES + 1)

    def cut_copy(k):
        p = (s + k) % PLACES
        if k == 0:
            return pltpu.make_async_copy(cutoffs.at[s], cut_all.at[s], cut_recv)
        return pltpu.make_async_remote_copy(
            src_ref=cutoffs.at[p],
            dst_ref=cut_all.at[s],
            send_sem=cut_send,
            recv_sem=cut_recv,
            device_id=(p, f),
            device_id_type=MESH_ID,
        )

    def in_copy(i, k):
        p = (s + k) % PLACES
        src = x.at[:, pl.ds(pl.multiple_of((p * CHUNKS + i) * GROUP, GROUP), GROUP), :]
        dst = inb.at[i, :, pl.ds(pl.multiple_of(s * GROUP, GROUP), GROUP), :]
        if k == 0:
            return pltpu.make_async_copy(src, dst, in_recv.at[i])
        return pltpu.make_async_remote_copy(
            src_ref=src,
            dst_ref=dst,
            send_sem=in_send,
            recv_sem=in_recv.at[i],
            device_id=(p, f),
            device_id_type=MESH_ID,
        )

    def halo_copy(i, side):
        if side == 0:
            src, dst, near = inb.at[i, :, :, pl.ds(COLS - SIDE, SIDE)], left.at[i], f_right
        else:
            src, dst, near = inb.at[i, :, :, pl.ds(0, SIDE)], right.at[i], f_left
        return pltpu.make_async_remote_copy(
            src_ref=src,
            dst_ref=dst,
            send_sem=halo_send,
            recv_sem=halo_recv.at[i],
            device_id=(s, near),
            device_id_type=MESH_ID,
        )

    def out_copy(i, k):
        p = (s + k) % PLACES
        src = outb.at[i, :, pl.ds(pl.multiple_of(p * GROUP, GROUP), GROUP), :]
        dst = back.at[:, s * CHUNKS + i]
        if k == 0:
            return pltpu.make_async_copy(src, dst, out_recv.at[i])
        return pltpu.make_async_remote_copy(
            src_ref=src,
            dst_ref=dst,
            send_sem=out_send,
            recv_sem=out_recv.at[i],
            device_id=(p, f),
            device_id_type=MESH_ID,
        )

    def tail_copy(h, k):
        p = (s + k) % PLACES
        src = outb.at[LAST, :, pl.ds(pl.multiple_of(p * GROUP + h * 8, 8), 8), :]
        dst = landed.at[:, pl.ds(pl.multiple_of(s * GROUP + h * 8, 8), 8), :]
        if k == 0:
            return pltpu.make_async_copy(src, dst, tail_recv.at[h])
        return pltpu.make_async_remote_copy(
            src_ref=src,
            dst_ref=dst,
            send_sem=tail_send,
            recv_sem=tail_recv.at[h],
            device_id=(p, f),
            device_id_type=MESH_ID,
        )

    def wait_for(sem, like):
        pltpu.make_async_copy(like, like, sem).wait()

    others = pl.ds(0, LANES - GROUP)

    order = (4, 3, 5, 2, 6, 1, 7, 0)
    def start_in(i, carry):
        for k in order:
            in_copy(i, k).start()
        return carry

    start_in(0, 0)
    for k in order:
        cut_copy(k).start()
    lax.fori_loop(1, CHUNKS, start_in, 0)

    fetches = [
        pltpu.make_async_copy(src, dst, small_sem.at[j])
        for j, (src, dst) in enumerate(
            (
                (small_5, angles),
                (small_4, drive_bits),
                (small_0, coupling_first),
                (small_1, coupling_second),
                (small_2, frozen_coupling),
                (small_3, frozen_bits),
            )
        )
    ]
    for fetch in fetches:
        fetch.start()
    for fetch in fetches:
        fetch.wait()
    fill_rotations(angles, drive_bits, rot)
    fill_mixer(rot, mix_hi, mix_lo)
    fill_diagonal(f, diag)
    wait_for(cut_recv, cut_all)

    def forward(i):
        wait_for(in_recv.at[i], inb.at[i])
        halo_copy(i, 0).start()
        halo_copy(i, 1).start()

    for i in range(AHEAD):
        forward(i)

    def series_step(k, i, coef):
        link, low_side, high_side = coef
        source_re, source_im = (odd_re, odd_im) if k % 2 == 0 else (even_re, even_im)
        target_re, target_im = (even_re, even_im) if k % 2 == 0 else (odd_re, odd_im)
        start = HALO - k
        groups = -(-(OWN + 2 * k) // 4)

        def group(g, carry):
            n0 = start + 4 * g

            def tile(ref, j, t):
                return ref[pl.ds(pl.multiple_of((n0 + j) * 16 + t * 8, 8), 8), :]

            steps = [ladder[pl.ds(n0 + j, 8, stride=0), :] for j in range(5)]
            diagonal = [[tile(diag, j, t) for t in range(2)] for j in range(4)]
            for source, target, vec, sign, y in (
                (source_im, target_re, vec_re, 1, y_re),
                (source_re, target_im, vec_im, -1, y_im),
            ):
                p = [[tile(source, j, t) for t in range(2)] for j in range(-1, 5)]
                for j in range(4):
                    for t in range(2):
                        own = p[j + 1][t]
                        other = p[j + 1][1 - t]
                        far = pltpu.roll(other, 1 if t == 0 else 7, axis=0)
                        applied = (
                            diagonal[j][t] * own
                            + link * other
                            + (low_side if t == 0 else high_side) * far
                            + (steps[j] * p[j][t] + steps[j + 1] * p[j + 2][t])
                        )
                        if k == 0:
                            applied = 0.5 * applied
                        kept = OMEGA[k] * tile(vec, j, t)
                        if k < DEGREE - 1:
                            kept = kept + tile(target, j, t)
                        value = kept + applied if sign > 0 else kept - applied
                        if k == 0:
                            row = (n0 + j - HALO) * 16 + t
                            y[pl.ds(row, 8, stride=2), :] = value
                        else:
                            target[pl.ds(pl.multiple_of((n0 + j) * 16 + t * 8, 8), 8), :] = value
            return carry

        lax.fori_loop(0, groups, group, 0)

    def chunk(i, carry):
        strength_first, strength_second = strengths(
            i, s, coupling_first, coupling_second, frozen_coupling, frozen_bits
        )
        cut = jnp.zeros((8, 128), jnp.int32)
        lane_place = iota((8, 128), 1) >> 4
        for q in range(PLACES):
            row = jnp.broadcast_to(cut_all[q], (8, 128))
            turned = pltpu.roll(row, ((q + 8 - i) * GROUP) % 128, axis=1)
            cut = jnp.where(lane_place == q, turned, cut)
        for block in range(9):
            level = f * OWN - HALO + block * 8 + iota((8, 128), 0)
            root = jnp.sqrt(jnp.maximum(level, 0).astype(jnp.float32) / FA)
            ladder[pl.ds(block * 8, 8), :] = jnp.where(
                (level >= 1) & (level < cut), 2.0 * strength_first * root, 0.0
            )
        sub = iota((8, 128), 0).astype(jnp.float32)
        double = 2.0 * strength_second
        link = double * jnp.sqrt((2.0 * sub + 1.0) / FB)
        low_side = double * jnp.sqrt(2.0 * sub / FB)
        high_side = jnp.where(sub < 7.0, double * jnp.sqrt((2.0 * sub + 2.0) / FB), 0.0)

        wait_for(halo_recv.at[i], inb.at[i])

        for part, natural in ((0, nat_re), (1, nat_im)):
            for b in range(8):
                if b < 2:
                    piece = left[i, part, :, b * 128 : (b + 1) * 128]
                elif b < 6:
                    piece = inb[i, part, :, (b - 2) * 128 : (b - 1) * 128]
                else:
                    piece = right[i, part, :, (b - 6) * 128 : (b - 5) * 128]
                natural[b * 128 : (b + 1) * 128, :] = piece.T

        def first_term(n, c):
            for natural, vec, even in ((nat_re, vec_re, even_re), (nat_im, vec_im, even_im)):
                for j in range(4):
                    for t in range(2):
                        value = natural[pl.ds((n * 4 + j) * 16 + t, 8, stride=2), :]
                        place = pl.ds(pl.multiple_of((n * 4 + j) * 16 + t * 8, 8), 8)
                        vec[place, :] = value
                        even[place, :] = OMEGA[DEGREE] * value
            return c

        lax.fori_loop(0, LEVELS // 4, first_term, 0)
        for k in range(DEGREE - 1, -1, -1):
            series_step(k, i, (link, low_side, high_side))

        y = jnp.concatenate([y_re[...], y_im[...]], axis=1)
        y_hi = y.astype(jnp.bfloat16)
        y_lo = (y - y_hi.astype(jnp.float32)).astype(jnp.bfloat16)

        def product(a, b):
            return lax.dot_general(
                a, b, (((1,), (1,)), ((), ())), preferred_element_type=jnp.float32
            )

        mixed = (
            product(mix_hi[...], y_hi) + product(mix_hi[...], y_lo) + product(mix_lo[...], y_hi)
        )
        outb[i, 0] = mixed[:LANES]
        outb[i, 1] = mixed[LANES:]

        @pl.when(i < LAST)
        def _():
            for k in order:
                out_copy(i, k).start()

        @pl.when(i == LAST)
        def _():
            for h in range(HALVES):
                for k in order:
                    tail_copy(h, k).start()

        @pl.when(i < CHUNKS - AHEAD)
        def _():
            forward(i + AHEAD)

        return carry

    lax.fori_loop(0, CHUNKS, chunk, 0)

    def turn(bit):
        return rot[3 * bit], rot[3 * bit + 1], rot[3 * bit + 2]

    for place in range(9):
        coef_out[2 * CHUNKS + place] = rot[21 + place]
    for i in range(CHUNKS):
        real = jnp.ones((8, 128), jnp.float32)
        imag = jnp.zeros((8, 128), jnp.float32)
        for place in range(3):
            cosine, driven, kept = turn(4 + place)
            if (i >> place) & 1:
                real, imag = real * cosine, imag * cosine
            else:
                real, imag = imag * kept - real * driven, -real * kept - imag * driven
        coef_out[i] = real
        coef_out[CHUNKS + i] = imag

    def spot(q, i, half, col):
        return (
            q * CHUNKS + i,
            pl.ds(pl.multiple_of(half * 8, 8), 8),
            pl.ds(pl.multiple_of(col * 128, 128), 128),
        )

    def rotate_places(i, carry):
        wait_for(out_recv.at[i], inb.at[i])

        def unit(u, c):
            half, col = u // COL_TILES, u % COL_TILES
            spots = [spot(q, i, half, col) for q in range(PLACES)]
            real = [back[0, g, r, l] for g, r, l in spots]
            imag = [back[1, g, r, l] for g, r, l in spots]
            real, imag = butterfly(real, imag, [(place, turn(7 + place)) for place in range(3)])
            for q, (g, r, l) in enumerate(spots):
                back[0, g, r, l] = real[q]
                back[1, g, r, l] = imag[q]
            return c

        lax.fori_loop(0, 2 * COL_TILES, unit, 0)
        return carry

    lax.fori_loop(0, LAST, rotate_places, 0)

    def rotate_chunks(q, carry):
        def unit(u, c):
            half, col = u // COL_TILES, u % COL_TILES
            spots = [spot(q, i, half, col) for i in range(CHUNKS)]
            zero = jnp.zeros((8, 128), jnp.float32)
            real = [back[0, g, r, l] for g, r, l in spots[:LAST]] + [zero]
            imag = [back[1, g, r, l] for g, r, l in spots[:LAST]] + [zero]
            real, imag = butterfly(real, imag, [(place, turn(4 + place)) for place in range(3)])
            for i, (g, r, l) in enumerate(spots):
                back[0, g, r, l] = real[i]
                back[1, g, r, l] = imag[i]
            return c

        lax.fori_loop(0, 2 * COL_TILES, unit, 0)
        return carry

    lax.fori_loop(0, PLACES, rotate_chunks, 0)

    wait_for(cut_send, cut_all.at[pl.ds(0, PLACES - 1)])
    wait_for(in_send, inb.at[:, :, others, :])
    wait_for(halo_send, inb)
    wait_for(out_send, inb.at[pl.ds(0, LAST), :, others, :])

    for h in range(HALVES):
        wait_for(tail_recv.at[h], landed.at[:, pl.ds(0, LANES // HALVES), :])
        if h < HALVES - 1:

            def finish(col, carry):
                finish_tile(landed, back, back, coef_out, h, h, col)
                return carry

            lax.fori_loop(0, COL_TILES, finish, 0)
    wait_for(tail_send, landed.at[:, others, :])


def finish_tile(landed, partial, done, coef, half, target, col):
    cols = pl.ds(pl.multiple_of(col * 128, 128), 128)
    rows = [pl.ds(q * GROUP + half * 8, 8) for q in range(PLACES)]
    real = [landed[0, r, cols] for r in rows]
    imag = [landed[1, r, cols] for r in rows]
    base = 2 * CHUNKS
    turns = [(place, tuple(coef[base + 3 * place + e] for e in range(3))) for place in range(3)]
    real, imag = butterfly(real, imag, turns)
    source, place = pl.ds(half * 8, 8), pl.ds(target * 8, 8)
    for i in range(CHUNKS):
        k_real, k_imag = coef[i], coef[CHUNKS + i]
        for q in range(PLACES):
            g = q * CHUNKS + i
            new_real = partial[0, g, source, cols] + (k_real * real[q] - k_imag * imag[q])
            new_imag = partial[1, g, source, cols] + (k_real * imag[q] + k_imag * real[q])
            done[0, g, place, cols] = new_real
            done[1, g, place, cols] = new_imag


def last_kernel(back, landed, coef, out, done, ready_sem, done_sem):
    ready = (HALVES - 1) * 8
    parts = []
    for j in range(4):
        groups = pl.ds(j * 16, 16)
        parts.append(
            pltpu.make_async_copy(
                back.at[:, groups, pl.ds(0, ready), :],
                out.at[:, groups, pl.ds(0, ready), :],
                ready_sem,
            )
        )
    for part in parts:
        part.start()

    def store_copy(col):
        cols = pl.ds(pl.multiple_of(col * 128, 128), 128)
        return pltpu.make_async_copy(
            done.at[:, :, :, cols], out.at[:, :, pl.ds(ready, 8), cols], done_sem
        )

    def finish(col, carry):
        finish_tile(landed, back, done, coef, HALVES - 1, 0, col)
        store_copy(col).start()
        return carry

    lax.fori_loop(0, COL_TILES, finish, 0)
    first = back.at[:, :, pl.ds(0, ready), :]
    pltpu.make_async_copy(first, first, ready_sem).wait()
    pltpu.make_async_copy(done, done, done_sem).wait()


def per_device(
    amplitudes,
    cutoffs,
    coupling_first,
    coupling_second,
    frozen_coupling,
    frozen_bits,
    drive_bits,
    angles,
):
    f32 = jnp.float32
    padded = pltpu.VMEM((PADDED * FB, LANES), f32)
    dma = pltpu.SemaphoreType.DMA
    vmem = pl.BlockSpec(memory_space=pltpu.VMEM)
    back, landed, coef = pl.pallas_call(
        kernel,
        name="evolve_and_rotate",
        out_shape=[
            pltpu.VMEM((2, PLACES * CHUNKS, GROUP, COLS), f32),
            pltpu.VMEM((2, LANES, COLS), f32),
            pltpu.VMEM((2 * CHUNKS + 9, 8, 128), f32),
        ],
        in_specs=[
            pl.BlockSpec(memory_space=pl.ANY),
        ]
        * 8,
        out_specs=[vmem, vmem, vmem],
        scratch_shapes=[
            pltpu.VMEM((CHUNKS, 2, LANES, COLS), f32),
            pltpu.VMEM((PLACES, 1, 128), jnp.int32),
            pltpu.VMEM((CHUNKS, 2, LANES, SIDE), f32),
            pltpu.VMEM((CHUNKS, 2, LANES, SIDE), f32),
            pltpu.VMEM((LEVELS * FB, LANES), f32),
            pltpu.VMEM((LEVELS * FB, LANES), f32),
            padded,
            padded,
            padded,
            padded,
            padded,
            padded,
            pltpu.VMEM((COLS, LANES), f32),
            pltpu.VMEM((COLS, LANES), f32),
            padded,
            pltpu.VMEM((72, LANES), f32),
            pltpu.VMEM((3 * SPINS, 8, 128), f32),
            pltpu.VMEM((2 * LANES, 2 * LANES), jnp.bfloat16),
            pltpu.VMEM((2 * LANES, 2 * LANES), jnp.bfloat16),
            pltpu.VMEM((CHUNKS, 2, LANES, COLS), f32),
            dma,
            dma((CHUNKS,)),
            dma,
            dma,
            dma,
            dma((CHUNKS,)),
            dma,
            dma((LAST,)),
            dma,
            dma((HALVES,)),
            pltpu.SMEM((SPINS,), f32),
            pltpu.SMEM((SPINS,), f32),
            pltpu.SMEM((FROZEN,), f32),
            pltpu.SMEM((FROZEN,), jnp.int32),
            pltpu.SMEM((SPINS,), jnp.int32),
            pltpu.SMEM((SPINS,), f32),
            dma((6,)),
        ],
        compiler_params=pltpu.CompilerParams(
            collective_id=0, has_side_effects=True, vmem_limit_bytes=62_100_000
        ),
    )(
        amplitudes,
        cutoffs.reshape(PLACES, 1, 128),
        coupling_first,
        coupling_second,
        frozen_coupling,
        frozen_bits,
        drive_bits,
        angles,
    )
    rotated = pl.pallas_call(
        last_kernel,
        name="rotate_last",
        out_shape=jax.ShapeDtypeStruct((2, PLACES * CHUNKS, GROUP, COLS), f32),
        in_specs=[vmem, vmem, vmem],
        out_specs=pl.BlockSpec(memory_space=pl.ANY),
        scratch_shapes=[
            pltpu.VMEM((2, PLACES * CHUNKS, 8, COLS), f32),
            dma,
            dma,
        ],
        compiler_params=pltpu.CompilerParams(vmem_limit_bytes=16 << 20),
    )(back, landed, coef)
    return rotated.reshape(amplitudes.shape)


def solution(mesh):
    placed = (P(None, "spin", "fock"), P("spin"), P(), P(), P(), P(), P(), P())
    return jax.shard_map(
        per_device, mesh=mesh, in_specs=placed, out_specs=P(None, "spin", "fock"), check_vma=False
    )
```
